1024 devices in a mesh: seq: 8 (over x, core), grp: 16 (over z), head: 8 (over y).
Axes of the slice: x: 4, y: 8, z: 16, core: 2. Of those that a mesh axis runs over, the one named last changes fastest.
Arguments:
- query_feat: bfloat16 [16, 8, 512, 6144], P('grp', 'seq', None, 'head'), may hold values from -6 to 6
- key_feat: bfloat16 [16, 8, 512, 6144], P('grp', 'seq', None, 'head'), may hold values from -6 to 6
- value_feat: bfloat16 [16, 8, 512, 6144], P('grp', 'seq', None, 'head'), may hold values from -6 to 6
- norm_gain: float32 [6144], P('head'), may hold values from 0.5 to 1.5
Outputs:
- attended: bfloat16 [16, 8, 512, 6144], P('grp', 'seq', None, 'head')
The draws below stay inside these ranges and needn't reach their ends.
All inputs are finite; a program needn't handle non-finite values.
Results may differ from the reference program's by a relative error of at most 0.0049.
Values sent between devices are 32-bit elements; how exact they have to be, the bound alone decides.
A program may use at most 64 MiB of HBM per device.

```python
import jax
import jax.numpy as jnp
from jax import lax

HEADS = 48
DH = 128
BLK = 512
TOK_DEV = 512
GROUPS = 16
SHARDS = 8


def levels(stream_key, dims, pieces, smallest, high):
    def one(position, parts):
        draws = jax.random.uniform(jax.random.fold_in(jax.random.fold_in(stream_key, 6), position), (parts,), jnp.float32, smallest / len(pieces), high / len(pieces))
        return jnp.repeat(jnp.exp(draws), dims[position] // parts).reshape((-1,) + (1,) * (len(dims) - position - 1))

    loudness = one(*pieces[0])
    for cut in pieces[1:]:
        loudness = loudness * one(*cut)
    return loudness


def normal_values(rng, extent, spread, reach, pieces=(), held_as=jnp.bfloat16):
    entries = jax.random.normal(rng, extent, jnp.float32) * spread
    if len(pieces) > 0:
        entries = levels(rng, extent, pieces, -0.22, 0.18) * entries
    return jnp.clip(entries, min=-reach, max=reach).astype(held_as)


def setup_inputs(seed: int = 0) -> dict:
    splits = jax.random.split(jax.random.key(seed), 5)
    return {
        "query_feat": normal_values(splits[0], (GROUPS, SHARDS, TOK_DEV, HEADS * DH), 1.0, 6.0, ((0, 16), (1, 8), (3, 8))),
        "key_feat": normal_values(splits[1], (GROUPS, SHARDS, TOK_DEV, HEADS * DH), 1.0, 6.0, ((0, 16), (1, 8), (3, 8))),
        "value_feat": normal_values(splits[2], (GROUPS, SHARDS, TOK_DEV, HEADS * DH), 1.0, 6.0, ((0, 16), (1, 8), (3, 8))),
        "norm_gain": jnp.clip(1.0 + 0.1 * jax.random.normal(splits[3], (HEADS * DH,), jnp.float32), 0.5, 1.5),
    }


def reference(query_feat, key_feat, value_feat, norm_gain):
    total = GROUPS * SHARDS * TOK_DEV
    nblocks = total // BLK

    def split(array):
        return array.reshape(nblocks, BLK, HEADS, DH)
    causal = jnp.arange(BLK)[:, None] >= jnp.arange(BLK)[None, :]
    gain = norm_gain.astype(jnp.float32).reshape(HEADS, DH)

    def advance(state, block):
        queries, keys_in, values = block
        q_wide = queries.astype(jnp.float32)
        k_wide = keys_in.astype(jnp.float32)
        v_wide = values.astype(jnp.float32)
        scores = jnp.einsum('thd,shd->hts', q_wide, k_wide)
        scores = jnp.where(causal[None], scores, 0.0)
        scores = lax.optimization_barrier(scores.astype(jnp.bfloat16)).astype(jnp.float32)
        rounded = lax.optimization_barrier(state.astype(jnp.bfloat16)).astype(jnp.float32)
        mixed = jnp.einsum('hts,she->the', scores, v_wide) + jnp.einsum('thd,hde->the', q_wide, rounded)
        meansq = lax.optimization_barrier(jnp.mean(mixed * mixed, axis=-1, keepdims=True))
        result = (mixed * lax.rsqrt(meansq + 1e-05) * gain).astype(jnp.bfloat16)
        new_state = state + jnp.einsum('thd,the->hde', k_wide, v_wide)
        return (new_state, result)
    start = jnp.zeros((HEADS, DH, DH), jnp.float32)
    _, outputs = lax.scan(advance, start, (split(query_feat), split(key_feat), split(value_feat)))
    return outputs.reshape(GROUPS, SHARDS, TOK_DEV, HEADS * DH)
```

```python
import jax
import jax.numpy as jnp
from jax import lax
from jax.experimental import pallas as pl
from jax.experimental.pallas import tpu as pltpu
from jax.sharding import PartitionSpec as P

DH = 128
MESH = pl.DeviceIdType.MESH
HPC = 2
PIECE = 8


def take(sem, ref):
    pltpu.make_async_copy(ref, ref, sem).wait()


def body(nx, nz, owners, eps, q_hbm, k_hbm, v_hbm, gain_hbm, out_ref, qb, kb, vb, gain, mixed,
         kv, pk, ts, ra, gs, rz, ez, bz, cs, rf,
         in_sem, gain_sem, sc, rc, sa, rcv_a, s1, r1, s2, r2, s3, r3, s4, r4):
    seq, z = lax.axis_index("seq"), lax.axis_index("grp")
    core, x = lax.rem(seq, 2), seq // 2
    tokens, width = qb.shape
    chunks = width // (HPC * DH)
    half = DH
    slc = half // nx
    pieces = slc // PIECE

    def chip(dx):
        return {"seq": lax.rem(x + dx, nx) * 2 + core}

    def along(dz):
        return {"grp": lax.rem(z + dz, nz)}

    partner = {"seq": x * 2 + 1 - core}

    def remote(src, dst, send, recv, where):
        pltpu.make_async_remote_copy(
            src_ref=src, dst_ref=dst, send_sem=send, recv_sem=recv, device_id=where, device_id_type=MESH
        ).start()

    barrier = pltpu.get_barrier_semaphore()
    for dz in range(1, nz):
        pl.semaphore_signal(barrier, inc=1, device_id=along(dz), device_id_type=MESH)
    for dx in range(1, nx):
        pl.semaphore_signal(barrier, inc=1, device_id=chip(dx), device_id_type=MESH)
    pl.semaphore_signal(barrier, inc=1, device_id=partner, device_id_type=MESH)

    loads = []
    for i, (hbm, buf) in enumerate(((k_hbm, kb), (v_hbm, vb), (q_hbm, qb))):
        for n in range(chunks):
            cols = pl.ds(n * HPC * DH, HPC * DH)
            loads.append(pltpu.make_async_copy(hbm.at[:, cols], buf.at[:, cols], in_sem.at[i, n]))
    for n in range(chunks):
        loads[n].start()
        loads[chunks + n].start()
    for n in range(chunks):
        loads[2 * chunks + n].start()
    gain_load = pltpu.make_async_copy(gain_hbm, gain, gain_sem)
    gain_load.start()

    def head(h):
        return pl.ds(h * DH, DH)

    for n in range(chunks):
        loads[n].wait()
        loads[chunks + n].wait()
        for j in range(HPC):
            h = n * HPC + j
            kv[n, pl.ds(j * DH, DH), :] = lax.dot_general(
                kb[:, head(h)], vb[:, head(h)], (((0,), (0,)), ((), ())), preferred_element_type=jnp.float32
            )
        if n == 0:
            pl.semaphore_wait(barrier, nz - 1 + nx - 1 + 1)
        remote(kv.at[n], pk.at[n], sc.at[n], rc.at[n], partner)

    mine = pl.ds(core * half, half)
    for n in range(chunks):
        take(rc.at[n], pk.at[n])
        ts[n] = kv[n, mine, :] + pk[n, mine, :]
        for dx in (2, 1, 3):
            to = lax.rem(x + dx, nx)
            remote(ts.at[n, pl.ds(to * slc, slc)], ra.at[n, pl.ds(x * slc, slc)], sa.at[n], rcv_a.at[n], chip(dx))
        ra[n, pl.ds(x * slc, slc), :] = ts[n, pl.ds(x * slc, slc), :]

    for n in range(chunks):
        take(rcv_a.at[n], ra.at[n, pl.ds(0, (nx - 1) * slc)])
        total = ra[n, pl.ds(0, slc), :]
        for i in range(1, nx):
            total = total + ra[n, pl.ds(i * slc, slc), :]
        gs[n] = total
        for p in range(pieces):
            own = owners[n][p]

            @pl.when(z != own)
            def _():
                remote(gs.at[n, pl.ds(p * PIECE, PIECE)], rz.at[z], s1.at[n], r1, {"grp": own})

            @pl.when(z == own)
            def _():
                rz[own] = gs[n, pl.ds(p * PIECE, PIECE), :]

    rows = tokens // 2
    later = lax.broadcasted_iota(jnp.int32, (rows, rows), 0) >= lax.broadcasted_iota(jnp.int32, (rows, rows), 1)

    def local_attention(h):
        cut = head(h)
        for r in range(2):
            part = pl.ds(r * rows, rows)
            qr = qb[part, cut]
            own_scores = lax.dot_general(qr, kb[part, cut], (((1,), (1,)), ((), ())), preferred_element_type=jnp.float32)
            weights = jnp.where(later, own_scores, 0.0).astype(jnp.bfloat16)
            acc = jnp.dot(weights, vb[part, cut], preferred_element_type=jnp.float32)
            if r == 1:
                first = pl.ds(0, rows)
                full = lax.dot_general(qr, kb[first, cut], (((1,), (1,)), ((), ())), preferred_element_type=jnp.float32)
                acc = acc + jnp.dot(full.astype(jnp.bfloat16), vb[first, cut], preferred_element_type=jnp.float32)
            mixed[part, cut] = acc

    for n in range(chunks):
        loads[2 * chunks + n].wait()
    gain_load.wait()
    heads_here = chunks * HPC
    for h in range(heads_here // 2):
        local_attention(h)

    far_first = sorted(range(1, nz), key=lambda d: -min(d, nz - d))
    for n in range(chunks):
        for p in range(pieces):
            own = owners[n][p]

            @pl.when(z == own)
            def _():
                take(r1, rz.at[pl.ds(0, nz - 1)])
                before = jnp.zeros((PIECE, DH), jnp.float32)
                for i in range(nz):
                    ez[i] = before
                    before = before + rz[i]
                for dz in far_first:
                    to = (own + dz) % nz
                    remote(ez.at[to], bz.at[n, pl.ds(p * PIECE, PIECE)], s2, r2.at[n], {"grp": to})
                bz[n, pl.ds(p * PIECE, PIECE), :] = ez[own]

    for h in range(heads_here // 2, heads_here):
        local_attention(h)

    def owns(n):
        hit = z == owners[n][0]
        for p in range(1, pieces):
            hit = jnp.logical_or(hit, z == owners[n][p])
        return hit

    for n in range(chunks):
        @pl.when(owns(n))
        def _():
            take(r2.at[n], bz.at[n, pl.ds(0, (pieces - 1) * PIECE)])

        @pl.when(jnp.logical_not(owns(n)))
        def _():
            take(r2.at[n], bz.at[n])

        before = bz[n]
        for i in range(nx):
            cs[n, pl.ds(i * slc, slc), :] = before
            before = before + ra[n, pl.ds(i * slc, slc), :]
        land = pl.ds(core * half + x * slc, slc)
        for dx in (2, 1, 3):
            to = lax.rem(x + dx, nx)
            remote(cs.at[n, pl.ds(to * slc, slc)], rf.at[n, land], s3.at[n], r3.at[n], chip(dx))
        rf[n, land, :] = cs[n, pl.ds(x * slc, slc), :]

    for n in range(chunks):
        take(r3.at[n], rf.at[n, pl.ds(0, (nx - 1) * slc)])
        remote(rf.at[n, mine], rf.at[n, mine], s4.at[n], r4.at[n], partner)

    second = core == 1
    for n in range(chunks):
        take(r4.at[n], rf.at[n, pl.ds(0, half)])
        for j in range(HPC):
            h = n * HPC + j
            at = pl.ds(j * DH, DH)
            state = rf[n, at, :] + jnp.where(second, pk[n, at, :], 0.0)
            m = mixed[:, head(h)] + jnp.dot(
                qb[:, head(h)], state.astype(jnp.bfloat16), preferred_element_type=jnp.float32
            )
            meansq = jnp.mean(m * m, axis=-1, keepdims=True)
            out_ref[:, head(h)] = (m * lax.rsqrt(meansq + eps) * gain[head(h)].reshape(1, DH)).astype(jnp.bfloat16)

    for n in range(chunks):
        take(sc.at[n], kv.at[n])
        take(sa.at[n], ts.at[n, pl.ds(0, (nx - 1) * slc)])
        take(s3.at[n], cs.at[n, pl.ds(0, (nx - 1) * slc)])
        take(s4.at[n], rf.at[n, pl.ds(0, half)])

        @pl.when(owns(n))
        def _():
            take(s1.at[n], gs.at[n, pl.ds(0, (pieces - 1) * PIECE)])
            take(s2, ez.at[pl.ds(0, nz - 1)])

        @pl.when(jnp.logical_not(owns(n)))
        def _():
            take(s1.at[n], gs.at[n])


def per_device(query_feat, key_feat, value_feat, norm_gain):
    tokens, width = query_feat.shape[2:]
    nx, nz = lax.axis_size("seq") // 2, lax.axis_size("grp")
    chunks = width // (HPC * DH)
    pieces = DH // nx // PIECE
    owners = [[(n + nz // pieces * p) % nz for p in range(pieces)] for n in range(chunks)]
    half, slc = DH, DH // nx
    f32 = jnp.float32
    dma = pltpu.SemaphoreType.DMA

    def kernel(*refs):
        body(nx, nz, owners, 1e-05, *refs)

    hbm = pl.BlockSpec(memory_space=pltpu.HBM)
    vmem = pl.BlockSpec(memory_space=pltpu.VMEM)
    out = pl.pallas_call(
        kernel,
        out_shape=jax.ShapeDtypeStruct((tokens, width), jnp.bfloat16),
        in_specs=[hbm, hbm, hbm, hbm],
        out_specs=vmem,
        scratch_shapes=[
            pltpu.VMEM((tokens, width), jnp.bfloat16),
            pltpu.VMEM((tokens, width), jnp.bfloat16),
            pltpu.VMEM((tokens, width), jnp.bfloat16),
            pltpu.VMEM((width,), f32),
            pltpu.VMEM((tokens, width), f32),
            pltpu.VMEM((chunks, HPC * DH, DH), f32),
            pltpu.VMEM((chunks, HPC * DH, DH), f32),
            pltpu.VMEM((chunks, half, DH), f32),
            pltpu.VMEM((chunks, half, DH), f32),
            pltpu.VMEM((chunks, slc, DH), f32),
            pltpu.VMEM((nz, PIECE, DH), f32),
            pltpu.VMEM((nz, PIECE, DH), f32),
            pltpu.VMEM((chunks, slc, DH), f32),
            pltpu.VMEM((chunks, half, DH), f32),
            pltpu.VMEM((chunks, HPC * DH, DH), f32),
            dma((3, chunks)), dma,
            dma((chunks,)), dma((chunks,)),
            dma((chunks,)), dma((chunks,)),
            dma((chunks,)), dma,
            dma, dma((chunks,)),
            dma((chunks,)), dma((chunks,)),
            dma((chunks,)), dma((chunks,)),
        ],
        compiler_params=pltpu.CompilerParams(collective_id=0, has_side_effects=True, vmem_limit_bytes=48 * 1024 * 1024),
        name="prefix_attention",
    )(
        query_feat.reshape(tokens, width),
        key_feat.reshape(tokens, width),
        value_feat.reshape(tokens, width),
        norm_gain,
    )
    return out.reshape(query_feat.shape)


def solution(mesh):
    placed = (
        P("grp", "seq", None, "head"),
        P("grp", "seq", None, "head"),
        P("grp", "seq", None, "head"),
        P("head"),
    )
    return jax.shard_map(
        per_device,
        mesh=mesh,
        in_specs=placed,
        out_specs=P("grp", "seq", None, "head"),
        check_vma=False,
    )
```

```python
import jax
import jax.numpy as jnp
from jax import lax
from jax.experimental import pallas as pl
from jax.experimental.pallas import tpu as pltpu
from jax.sharding import PartitionSpec as P

DH = 128
MESH = pl.DeviceIdType.MESH
HPC = 2
REACH = 4


def take(sem, ref):
    pltpu.make_async_copy(ref, ref, sem).wait()


def body(nx, nz, eps, q_hbm, k_hbm, v_hbm, gain_hbm, out_ref, qb, kb, vb, gain, mixed,
         kv, pk, ts, ra, gs, rw, run, cs, rf,
         in_sem, gain_sem, sc, rc, sa, rcv_a, s1, r1, s3, r3, s4, r4):
    seq, z = lax.axis_index("seq"), lax.axis_index("grp")
    core, x = lax.rem(seq, 2), seq // 2
    tokens, width = qb.shape
    chunks = width // (HPC * DH)
    half = DH
    slc = half // nx
    rows = tokens // 2
    first = jnp.logical_and(jnp.logical_and(seq == 0, z == 0), lax.axis_index("head") == 0)

    def chip(dx):
        return {"seq": lax.rem(x + dx, nx) * 2 + core}

    def along(dz):
        return {"grp": lax.rem(z + dz, nz)}

    partner = {"seq": x * 2 + 1 - core}

    def remote(src, dst, send, recv, where):
        pltpu.make_async_remote_copy(
            src_ref=src, dst_ref=dst, send_sem=send, recv_sem=recv, device_id=where, device_id_type=MESH
        ).start()

    barrier = pltpu.get_barrier_semaphore()
    pl.semaphore_signal(barrier, inc=1, device_id=partner, device_id_type=MESH)
    for dx in range(1, nx):
        pl.semaphore_signal(barrier, inc=1, device_id=chip(dx), device_id_type=MESH)
    for d in range(1, REACH + 1):
        @pl.when(z >= d)
        def _():
            pl.semaphore_signal(barrier, inc=1, device_id={"grp": z - d}, device_id_type=MESH)

    def greeted():
        pl.semaphore_wait(barrier, 1 + nx - 1 + jnp.minimum(REACH, nz - 1 - z))

    loads = []
    for i, (hbm, buf) in enumerate(((k_hbm, kb), (v_hbm, vb), (q_hbm, qb))):
        for n in range(chunks):
            cols = pl.ds(n * HPC * DH, HPC * DH)
            loads.append(pltpu.make_async_copy(hbm.at[:, cols], buf.at[:, cols], in_sem.at[i, n]))
    for n in range(chunks):
        loads[n].start()
        loads[chunks + n].start()
    for n in range(chunks):
        loads[2 * chunks + n].start()
    gain_load = pltpu.make_async_copy(gain_hbm, gain, gain_sem)
    gain_load.start()

    def head(h):
        return pl.ds(h * DH, DH)

    later = lax.broadcasted_iota(jnp.int32, (rows, rows), 0) >= lax.broadcasted_iota(jnp.int32, (rows, rows), 1)

    def local_attention(h):
        cut = head(h)
        for r in range(2):
            part = pl.ds(r * rows, rows)
            qr = qb[part, cut]
            own_scores = lax.dot_general(qr, kb[part, cut], (((1,), (1,)), ((), ())), preferred_element_type=jnp.float32)
            weights = jnp.where(later, own_scores, 0.0).astype(jnp.bfloat16)
            acc = jnp.dot(weights, vb[part, cut], preferred_element_type=jnp.float32)
            if r == 1:
                first = pl.ds(0, rows)
                full = lax.dot_general(qr, kb[first, cut], (((1,), (1,)), ((), ())), preferred_element_type=jnp.float32)
                acc = acc + jnp.dot(full.astype(jnp.bfloat16), vb[first, cut], preferred_element_type=jnp.float32)
            mixed[part, cut] = acc

    def attend():
        for n in range(chunks):
            for j in range(HPC):
                local_attention(n * HPC + j)

    def exchange(n):
        remote(kv.at[n], pk.at[n], sc.at[n], rc.at[n], partner)

    @pl.when(first)
    def _():
        greeted()

    for n in range(chunks):
        loads[n].wait()
        loads[chunks + n].wait()
        for j in range(HPC):
            h = n * HPC + j
            kv[n, pl.ds(j * DH, DH), :] = lax.dot_general(
                kb[:, head(h)], vb[:, head(h)], (((0,), (0,)), ((), ())), preferred_element_type=jnp.float32
            )

        @pl.when(first)
        def _():
            exchange(n)

    for n in range(chunks):
        loads[2 * chunks + n].wait()
    gain_load.wait()
    for d in range(1, REACH + 1):
        @pl.when(z < d)
        def _():
            for n in range(chunks):
                rw[n, d - 1] = jnp.zeros((slc, DH), jnp.float32)

    @pl.when(jnp.logical_not(first))
    def _():
        attend()
        greeted()
        for n in range(chunks):
            exchange(n)

    mine = pl.ds(core * half, half)
    for n in range(chunks):
        take(rc.at[n], pk.at[n])
        ts[n] = kv[n, mine, :] + pk[n, mine, :]
        for dx in (2, 1, 3):
            to = lax.rem(x + dx, nx)
            remote(ts.at[n, pl.ds(to * slc, slc)], ra.at[n, pl.ds(x * slc, slc)], sa.at[n], rcv_a.at[n], chip(dx))
        ra[n, pl.ds(x * slc, slc), :] = ts[n, pl.ds(x * slc, slc), :]

    for n in range(chunks):
        take(rcv_a.at[n], ra.at[n, pl.ds(0, (nx - 1) * slc)])
        total = ra[n, pl.ds(0, slc), :]
        for i in range(1, nx):
            total = total + ra[n, pl.ds(i * slc, slc), :]
        gs[n] = total
        for d in range(1, REACH):
            @pl.when(z + d < nz)
            def _():
                remote(gs.at[n], rw.at[n, d - 1], s1.at[n, d - 1], r1.at[n, d - 1], {"grp": z + d})

    for n in range(chunks):
        for d in range(1, REACH + 1):
            @pl.when(z >= d)
            def _():
                take(r1.at[n, d - 1], rw.at[n, d - 1])

        before = rw[n, REACH - 1]
        for d in range(REACH - 1, 0, -1):
            before = before + rw[n, d - 1]
        run[n] = before + gs[n]

        @pl.when(z + REACH < nz)
        def _():
            remote(run.at[n], rw.at[n, REACH - 1], s1.at[n, REACH - 1], r1.at[n, REACH - 1], {"grp": z + REACH})

        for i in range(nx):
            cs[n, pl.ds(i * slc, slc), :] = before
            before = before + ra[n, pl.ds(i * slc, slc), :]
        land = pl.ds(core * half + x * slc, slc)
        for dx in (2, 1, 3):
            to = lax.rem(x + dx, nx)
            remote(cs.at[n, pl.ds(to * slc, slc)], rf.at[n, land], s3.at[n], r3.at[n], chip(dx))
        rf[n, land, :] = cs[n, pl.ds(x * slc, slc), :]

    for n in range(chunks):
        take(r3.at[n], rf.at[n, pl.ds(0, (nx - 1) * slc)])
        remote(rf.at[n, mine], rf.at[n, mine], s4.at[n], r4.at[n], partner)

    @pl.when(first)
    def _():
        attend()

    second = core == 1
    for n in range(chunks):
        take(r4.at[n], rf.at[n, pl.ds(0, half)])
        for j in range(HPC):
            h = n * HPC + j
            at = pl.ds(j * DH, DH)
            state = rf[n, at, :] + jnp.where(second, pk[n, at, :], 0.0)
            m = mixed[:, head(h)] + jnp.dot(
                qb[:, head(h)], state.astype(jnp.bfloat16), preferred_element_type=jnp.float32
            )
            meansq = jnp.mean(m * m, axis=-1, keepdims=True)
            out_ref[:, head(h)] = (m * lax.rsqrt(meansq + eps) * gain[head(h)].reshape(1, DH)).astype(jnp.bfloat16)

    for n in range(chunks):
        take(sc.at[n], kv.at[n])
        take(sa.at[n], ts.at[n, pl.ds(0, (nx - 1) * slc)])
        take(s3.at[n], cs.at[n, pl.ds(0, (nx - 1) * slc)])
        take(s4.at[n], rf.at[n, pl.ds(0, half)])

        for d in range(1, REACH + 1):
            @pl.when(z + d < nz)
            def _():
                take(s1.at[n, d - 1], gs.at[n])


def per_device(query_feat, key_feat, value_feat, norm_gain):
    tokens, width = query_feat.shape[2:]
    nx, nz = lax.axis_size("seq") // 2, lax.axis_size("grp")
    chunks = width // (HPC * DH)
    half, slc = DH, DH // nx
    f32 = jnp.float32
    dma = pltpu.SemaphoreType.DMA

    def kernel(*refs):
        body(nx, nz, 1e-05, *refs)

    hbm = pl.BlockSpec(memory_space=pltpu.HBM)
    vmem = pl.BlockSpec(memory_space=pltpu.VMEM)
    out = pl.pallas_call(
        kernel,
        out_shape=jax.ShapeDtypeStruct((tokens, width), jnp.bfloat16),
        in_specs=[hbm, hbm, hbm, hbm],
        out_specs=vmem,
        scratch_shapes=[
            pltpu.VMEM((tokens, width), jnp.bfloat16),
            pltpu.VMEM((tokens, width), jnp.bfloat16),
            pltpu.VMEM((tokens, width), jnp.bfloat16),
            pltpu.VMEM((width,), f32),
            pltpu.VMEM((tokens, width), f32),
            pltpu.VMEM((chunks, HPC * DH, DH), f32),
            pltpu.VMEM((chunks, HPC * DH, DH), f32),
            pltpu.VMEM((chunks, half, DH), f32),
            pltpu.VMEM((chunks, half, DH), f32),
            pltpu.VMEM((chunks, slc, DH), f32),
            pltpu.VMEM((chunks, REACH, slc, DH), f32),
            pltpu.VMEM((chunks, slc, DH), f32),
            pltpu.VMEM((chunks, half, DH), f32),
            pltpu.VMEM((chunks, HPC * DH, DH), f32),
            dma((3, chunks)), dma,
            dma((chunks,)), dma((chunks,)),
            dma((chunks,)), dma((chunks,)),
            dma((chunks, REACH)), dma((chunks, REACH)),
            dma((chunks,)), dma((chunks,)),
            dma((chunks,)), dma((chunks,)),
        ],
        compiler_params=pltpu.CompilerParams(collective_id=0, has_side_effects=True, vmem_limit_bytes=48 * 1024 * 1024),
        name="prefix_attention",
    )(
        *(
            pltpu.with_memory_space_constraint(a, pltpu.HBM)
            for a in (
                query_feat.reshape(tokens, width),
                key_feat.reshape(tokens, width),
                value_feat.reshape(tokens, width),
                norm_gain,
            )
        )
    )
    return out.reshape(query_feat.shape)


def solution(mesh):
    placed = (
        P("grp", "seq", None, "head"),
        P("grp", "seq", None, "head"),
        P("grp", "seq", None, "head"),
        P("head"),
    )
    return jax.shard_map(
        per_device,
        mesh=mesh,
        in_specs=placed,
        out_specs=P("grp", "seq", None, "head"),
        check_vma=False,
    )
```

```python
import jax
import jax.numpy as jnp
from jax import lax
from jax.experimental import pallas as pl
from jax.experimental.pallas import tpu as pltpu
from jax.sharding import PartitionSpec as P

DH = 128
MESH = pl.DeviceIdType.MESH
HPC = 2
REACH = 4
STEPS = ((0, 1), (1, 2), (2, REACH))


def take(sem, ref):
    pltpu.make_async_copy(ref, ref, sem).wait()


def body(nx, nz, eps, q_hbm, k_hbm, v_hbm, gain_hbm, out_ref, qb, kb, vb, gain, mixed,
         kv, pk, ts, ra, gs, rw, two, run, bf, lt, cs, rf,
         in_sem, gain_sem, sc, rc, sa, rcv_a, s1, r1, s3, r3, s4, r4, sl, rl, hello, word):
    seq, z = lax.axis_index("seq"), lax.axis_index("grp")
    core, x = lax.rem(seq, 2), seq // 2
    tokens, width = qb.shape
    chunks = width // (HPC * DH)
    half = HPC * DH // 2
    slc = half // nx
    rows = tokens // 2
    plane = lax.axis_index("head") == 0
    late = jnp.logical_and(plane, z == 0)
    first = jnp.logical_and(late, seq == 0)
    origin = jnp.where(plane, 1, 0)
    relay, end = REACH, nz - 1

    middle = 2 * relay
    split = middle + 3
    fans = ((relay, (middle, *range(relay + 1, middle))), (middle, range(middle + 1, split)), (end, range(split, end)))

    def feeds(d):
        return jnp.logical_and(z >= origin, z + d < nz)

    def chip(dx):
        return {"seq": lax.rem(x + dx, nx) * 2 + core}

    partner = {"seq": x * 2 + 1 - core}

    def remote(src, dst, send, recv, where):
        pltpu.make_async_remote_copy(
            src_ref=src, dst_ref=dst, send_sem=send, recv_sem=recv, device_id=where, device_id_type=MESH
        ).start()

    barrier = pltpu.get_barrier_semaphore()
    pl.semaphore_signal(barrier, inc=1, device_id=partner, device_id_type=MESH)
    for dx in range(1, nx):
        pl.semaphore_signal(barrier, inc=1, device_id=chip(dx), device_id_type=MESH)
    final = jnp.logical_and(plane, z == end)
    for there, to in ((z >= 1, z - 1), (feeds(1), z + 1), (late, end)):
        @pl.when(there)
        def _():
            pl.semaphore_signal(barrier, inc=1, device_id={"grp": to}, device_id_type=MESH)

    def greeted():
        pl.semaphore_wait(barrier, nx + jnp.minimum(jnp.maximum(z - origin, 0), 1) + jnp.minimum(nz - 1 - z, 1) + jnp.where(final, 1, 0))
        announce(0)

        @pl.when(final)
        def _():
            pl.semaphore_signal(word.at[1], inc=1, device_id={"grp": 0}, device_id_type=MESH)

        @pl.when(late)
        def _():
            pl.semaphore_signal(word.at[1], inc=1, device_id={"grp": 1}, device_id_type=MESH)

    def tell(i):
        pl.semaphore_signal(hello.at[i], inc=1, device_id={"grp": z - 1}, device_id_type=MESH)

    def announce(i):
        @pl.when(z > origin)
        def _():
            tell(i)

    def learn(i):
        @pl.when(z + 1 < nz)
        def _():
            pl.semaphore_wait(hello.at[i], 1)

    loads = []
    for i, (hbm, buf) in enumerate(((k_hbm, kb), (v_hbm, vb), (q_hbm, qb))):
        for n in range(chunks):
            cols = pl.ds(n * HPC * DH, HPC * DH)
            loads.append(pltpu.make_async_copy(hbm.at[:, cols], buf.at[:, cols], in_sem.at[i, n]))
    for n in range(chunks):
        loads[n].start()
        loads[chunks + n].start()
    for n in range(chunks):
        loads[2 * chunks + n].start()
    gain_load = pltpu.make_async_copy(gain_hbm, gain, gain_sem)
    gain_load.start()

    def head(h):
        return pl.ds(h * DH, DH)

    later = lax.broadcasted_iota(jnp.int32, (rows, rows), 0) >= lax.broadcasted_iota(jnp.int32, (rows, rows), 1)

    def local_attention(h):
        cut = head(h)
        for r in range(2):
            part = pl.ds(r * rows, rows)
            qr = qb[part, cut]
            own_scores = lax.dot_general(qr, kb[part, cut], (((1,), (1,)), ((), ())), preferred_element_type=jnp.float32)
            weights = jnp.where(later, own_scores, 0.0).astype(jnp.bfloat16)
            acc = jnp.dot(weights, vb[part, cut], preferred_element_type=jnp.float32)
            if r == 1:
                top = pl.ds(0, rows)
                full = lax.dot_general(qr, kb[top, cut], (((1,), (1,)), ((), ())), preferred_element_type=jnp.float32)
                acc = acc + jnp.dot(full.astype(jnp.bfloat16), vb[top, cut], preferred_element_type=jnp.float32)
            mixed[part, cut] = acc

    def attend():
        for n in range(chunks):
            for j in range(HPC):
                local_attention(n * HPC + j)

    def exchange(n):
        remote(kv.at[n], pk.at[n], sc.at[n], rc.at[n], partner)

    @pl.when(first)
    def _():
        greeted()

    for n in range(chunks):
        loads[n].wait()
        loads[chunks + n].wait()
        for j in range(HPC):
            h = n * HPC + j
            kv[n, pl.ds(j * DH, DH), :] = lax.dot_general(
                kb[:, head(h)], vb[:, head(h)], (((0,), (0,)), ((), ())), preferred_element_type=jnp.float32
            )

        @pl.when(first)
        def _():
            exchange(n)

    for n in range(chunks):
        loads[2 * chunks + n].wait()
    gain_load.wait()
    for i, d in STEPS:
        @pl.when(z - origin < d)
        def _():
            for n in range(chunks):
                rw[n, i] = jnp.zeros((slc, DH), jnp.float32)

    @pl.when(jnp.logical_and(late, jnp.logical_not(first)))
    def _():
        attend()

    @pl.when(jnp.logical_not(first))
    def _():
        greeted()
        for n in range(chunks):
            exchange(n)

    mine = pl.ds(core * half, half)
    for n in range(chunks):
        take(rc.at[n], pk.at[n])
        ts[n] = kv[n, mine, :] + pk[n, mine, :]
        for dx in (2, 1, 3):
            to = lax.rem(x + dx, nx)
            remote(ts.at[n, pl.ds(to * slc, slc)], ra.at[n, pl.ds(x * slc, slc)], sa.at[n], rcv_a.at[n], chip(dx))
        ra[n, pl.ds(x * slc, slc), :] = ts[n, pl.ds(x * slc, slc), :]

    @pl.when(jnp.logical_and(plane, z > split + 1))
    def _():
        pl.semaphore_wait(word.at[0], 1)

    @pl.when(jnp.logical_and(jnp.logical_and(plane, z > split), z < end))
    def _():
        pl.semaphore_signal(word.at[0], inc=1, device_id={"grp": z + 1}, device_id_type=MESH)

    for i in range(REACH - 2):
        learn(i)
        announce(i + 1)

    for n in range(chunks):
        take(rcv_a.at[n], ra.at[n, pl.ds(0, (nx - 1) * slc)])
        total = ra[n, pl.ds(0, slc), :]
        for i in range(1, nx):
            total = total + ra[n, pl.ds(i * slc, slc), :]
        gs[n] = total
        @pl.when(feeds(1))
        def _():
            remote(gs.at[n], rw.at[n, 0], s1.at[n, 0], r1.at[n, 0], {"grp": z + 1})

        @pl.when(late)
        def _():
            if n == 0:
                pl.semaphore_wait(word.at[1], 1)
            for i, to in enumerate((relay, 1, end, *range(2, relay))):
                remote(gs.at[n], lt.at[n], sl.at[n, i], rl.at[n], {"grp": to})


    def pass_on(n, source, targets):
        @pl.when(z == source)
        def _():
            for i, to in enumerate(targets):
                remote(lt.at[n], lt.at[n], sl.at[n, i], rl.at[n], {"grp": to})

    @pl.when(final)
    def _():
        for n in range(chunks):
            take(rl.at[n], lt.at[n])
            pass_on(n, *fans[-1])

    for n in range(chunks):
        @pl.when(z - origin >= 1)
        def _():
            take(r1.at[n, 0], rw.at[n, 0])

        two[n] = gs[n] + rw[n, 0]

        @pl.when(feeds(2))
        def _():
            remote(two.at[n], rw.at[n, 1], s1.at[n, 1], r1.at[n, 1], {"grp": z + 2})

    @pl.when(jnp.logical_not(late))
    def _():
        attend()

    def hand_back(n, before):
        for i in range(nx):
            cs[n, pl.ds(i * slc, slc), :] = before
            before = before + ra[n, pl.ds(i * slc, slc), :]
        land = pl.ds(core * half + x * slc, slc)
        for dx in (2, 1, 3):
            to = lax.rem(x + dx, nx)
            remote(cs.at[n, pl.ds(to * slc, slc)], rf.at[n, land], s3.at[n], r3.at[n], chip(dx))
        rf[n, land, :] = cs[n, pl.ds(x * slc, slc), :]

    for n in range(chunks):
        for i, d in STEPS[1:]:
            @pl.when(z - origin >= d)
            def _():
                take(r1.at[n, i], rw.at[n, i])

        before = rw[n, 2] + rw[n, 1] + rw[n, 0]
        run[n] = before + gs[n]
        if n == 0:
            learn(REACH - 2)

        @pl.when(feeds(REACH))
        def _():
            remote(run.at[n], rw.at[n, 2], s1.at[n, 2], r1.at[n, 2], {"grp": z + REACH})

        bf[n] = before

        @pl.when(jnp.logical_not(plane))
        def _():
            hand_back(n, bf[n])

    @pl.when(plane)
    def _():
        @pl.when(z == 1)
        def _():
            pl.semaphore_wait(word.at[1], 1)
            for i in range(REACH - 1):
                tell(i)

        for n in range(chunks):
            @pl.when(jnp.logical_and(z >= 1, z < end))
            def _():
                take(rl.at[n], lt.at[n])
                for source, targets in fans[:-1]:
                    pass_on(n, source, targets)

            @pl.when(z >= 1)
            def _():
                bf[n] = bf[n] + lt[n]

            hand_back(n, bf[n])

    for n in range(chunks):
        take(r3.at[n], rf.at[n, pl.ds(0, (nx - 1) * slc)])
        remote(rf.at[n, mine], rf.at[n, mine], s4.at[n], r4.at[n], partner)

    @pl.when(first)
    def _():
        attend()

    second = core == 1
    for n in range(chunks):
        take(r4.at[n], rf.at[n, pl.ds(0, half)])
        for j in range(HPC):
            h = n * HPC + j
            at = pl.ds(j * DH, DH)
            state = rf[n, at, :] + jnp.where(second, pk[n, at, :], 0.0)
            m = mixed[:, head(h)] + jnp.dot(
                qb[:, head(h)], state.astype(jnp.bfloat16), preferred_element_type=jnp.float32
            )
            meansq = jnp.mean(m * m, axis=-1, keepdims=True)
            out_ref[:, head(h)] = (m * lax.rsqrt(meansq + eps) * gain[head(h)].reshape(1, DH)).astype(jnp.bfloat16)

    for n in range(chunks):
        take(sc.at[n], kv.at[n])
        take(sa.at[n], ts.at[n, pl.ds(0, (nx - 1) * slc)])
        take(s3.at[n], cs.at[n, pl.ds(0, (nx - 1) * slc)])
        take(s4.at[n], rf.at[n, pl.ds(0, half)])

        for i, d in STEPS:
            @pl.when(feeds(d))
            def _():
                take(s1.at[n, i], gs.at[n])

        @pl.when(late)
        def _():
            for i in range(relay + 1):
                take(sl.at[n, i], lt.at[n])

        for source, targets in fans:
            @pl.when(jnp.logical_and(plane, z == source))
            def _():
                for i in range(len(targets)):
                    take(sl.at[n, i], lt.at[n])


def per_device(query_feat, key_feat, value_feat, norm_gain):
    tokens, width = query_feat.shape[2:]
    nx, nz = lax.axis_size("seq") // 2, lax.axis_size("grp")
    chunks = width // (HPC * DH)
    half = HPC * DH // 2
    slc = half // nx
    f32 = jnp.float32
    dma = pltpu.SemaphoreType.DMA

    def kernel(*refs):
        body(nx, nz, 1e-05, *refs)

    hbm = pl.BlockSpec(memory_space=pltpu.HBM)
    vmem = pl.BlockSpec(memory_space=pltpu.VMEM)
    out = pl.pallas_call(
        kernel,
        out_shape=jax.ShapeDtypeStruct((tokens, width), jnp.bfloat16),
        in_specs=[hbm, hbm, hbm, hbm],
        out_specs=vmem,
        scratch_shapes=[
            pltpu.VMEM((tokens, width), jnp.bfloat16),
            pltpu.VMEM((tokens, width), jnp.bfloat16),
            pltpu.VMEM((tokens, width), jnp.bfloat16),
            pltpu.VMEM((width,), f32),
            pltpu.VMEM((tokens, width), f32),
            pltpu.VMEM((chunks, HPC * DH, DH), f32),
            pltpu.VMEM((chunks, HPC * DH, DH), f32),
            pltpu.VMEM((chunks, half, DH), f32),
            pltpu.VMEM((chunks, half, DH), f32),
            pltpu.VMEM((chunks, slc, DH), f32),
            pltpu.VMEM((chunks, len(STEPS), slc, DH), f32),
            pltpu.VMEM((chunks, slc, DH), f32),
            pltpu.VMEM((chunks, slc, DH), f32),
            pltpu.VMEM((chunks, slc, DH), f32),
            pltpu.VMEM((chunks, slc, DH), f32),
            pltpu.VMEM((chunks, half, DH), f32),
            pltpu.VMEM((chunks, HPC * DH, DH), f32),
            dma((3, chunks)), dma,
            dma((chunks,)), dma((chunks,)),
            dma((chunks,)), dma((chunks,)),
            dma((chunks, len(STEPS))), dma((chunks, len(STEPS))),
            dma((chunks,)), dma((chunks,)),
            dma((chunks,)), dma((chunks,)),
            dma((chunks, nz)), dma((chunks,)),
            pltpu.SemaphoreType.REGULAR((REACH - 1,)),
            pltpu.SemaphoreType.REGULAR((2,)),
        ],
        compiler_params=pltpu.CompilerParams(collective_id=0, has_side_effects=True, vmem_limit_bytes=48 * 1024 * 1024),
        name="prefix_attention",
    )(
        *(
            pltpu.with_memory_space_constraint(a, pltpu.HBM)
            for a in (
                query_feat.reshape(tokens, width),
                key_feat.reshape(tokens, width),
                value_feat.reshape(tokens, width),
                norm_gain,
            )
        )
    )
    return out.reshape(query_feat.shape)


def solution(mesh):
    placed = (
        P("grp", "seq", None, "head"),
        P("grp", "seq", None, "head"),
        P("grp", "seq", None, "head"),
        P("head"),
    )
    return jax.shard_map(
        per_device,
        mesh=mesh,
        in_specs=placed,
        out_specs=P("grp", "seq", None, "head"),
        check_vma=False,
    )
```

```python
import jax
import jax.numpy as jnp
from jax import lax
from jax.experimental import pallas as pl
from jax.experimental.pallas import tpu as pltpu
from jax.sharding import PartitionSpec as P

DH = 128
MESH = pl.DeviceIdType.MESH
HPC = 2
REACH = 4
FILL = (0, 2, 4, 6)


def take(sem, ref):
    pltpu.make_async_copy(ref, ref, sem).wait()


def body(nx, nz, eps, q_hbm, k_hbm, v_hbm, gain_hbm, out_ref, qb, kb, vb, gain, mixed,
         kv, pk, ts, ra, gs, rw, run, bf, lt, lk, cs, rf,
         in_sem, gain_sem, sc, rc, sa, rcv_a, s1, r1, s3, r3, s4, r4, sl, rl, sk, rk, hello, word, enter):
    seq, z = lax.axis_index("seq"), lax.axis_index("grp")
    core, x = lax.rem(seq, 2), seq // 2
    tokens, width = qb.shape
    chunks = width // (HPC * DH)
    half = HPC * DH // 2
    slc = half // nx
    rows = tokens // 2
    plane = lax.axis_index("head") == 0
    late = jnp.logical_and(plane, z == 0)
    first = jnp.logical_and(late, seq == 0)
    mate = jnp.logical_and(late, seq == 1)
    others = jnp.logical_and(late, seq > 1)
    row, odd = jnp.logical_and(others, core == 0), jnp.logical_and(others, core == 1)
    origin = jnp.where(plane, 1, 0)
    relay, end = REACH, nz - 1
    final = jnp.logical_and(plane, z == end)

    middle = 2 * relay
    split = middle + 3
    fans = ((relay, (middle, *range(relay + 1, middle))), (middle, range(middle + 1, split)), (end, range(split, end)))

    place = lax.rem(z, REACH)
    tail = place == REACH - 1

    def inside(d):
        return jnp.logical_and(feeds(d), place + d < REACH)

    def feeds(d):
        return jnp.logical_and(z >= origin, z + d < nz)

    def chip(dx):
        return {"seq": lax.rem(x + dx, nx) * 2 + core}

    partner = {"seq": x * 2 + 1 - core}

    def remote(src, dst, send, recv, where):
        pltpu.make_async_remote_copy(
            src_ref=src, dst_ref=dst, send_sem=send, recv_sem=recv, device_id=where, device_id_type=MESH
        ).start()

    barrier = pltpu.get_barrier_semaphore()
    pl.semaphore_signal(barrier, inc=1, device_id=partner, device_id_type=MESH)

    @pl.when(jnp.logical_not(first))
    def _():
        for dx in range(1, nx):
            pl.semaphore_signal(barrier, inc=1, device_id=chip(dx), device_id_type=MESH)

    notes = [(feeds(d), z + d) for d in range(1, REACH + 1)]
    @pl.when(odd)
    def _():
        pl.semaphore_signal(barrier, inc=1, device_id={"seq": 0}, device_id_type=MESH)

    notes += [(jnp.logical_and(plane, jnp.logical_and(z >= 1, z <= relay)), 0), (late, end)]
    for there, to in notes:
        @pl.when(there)
        def _():
            pl.semaphore_signal(barrier, inc=1, device_id={"grp": to}, device_id_type=MESH)

    def greeted():
        behind = jnp.minimum(jnp.maximum(z - origin, 0), REACH)
        behind = behind + jnp.where(first, nx - 1, 0) - jnp.where(row, 1, 0)
        pl.semaphore_wait(barrier, nx + behind + jnp.where(late, relay, 0) + jnp.where(final, 1, 0))
        for d in range(1, REACH + 1):
            @pl.when(z - d >= origin)
            def _():
                pl.semaphore_signal(hello.at[d - 1], inc=1, device_id={"grp": z - d}, device_id_type=MESH)

        @pl.when(final)
        def _():
            pl.semaphore_signal(word, inc=1, device_id={"grp": 0}, device_id_type=MESH)

        @pl.when(first)
        def _():
            for i in range(1, nx):
                pl.semaphore_signal(enter, inc=1, device_id={"seq": 2 * i}, device_id_type=MESH)

    def learn(d, wanted):
        @pl.when(jnp.logical_and(feeds(d), wanted))
        def _():
            pl.semaphore_wait(hello.at[d - 1], 1)

    loads = []
    for i, (hbm, buf) in enumerate(((k_hbm, kb), (v_hbm, vb), (q_hbm, qb))):
        for n in range(chunks):
            cols = pl.ds(n * HPC * DH, HPC * DH)
            loads.append(pltpu.make_async_copy(hbm.at[:, cols], buf.at[:, cols], in_sem.at[i, n]))
    for n in range(chunks):
        loads[n].start()
        loads[chunks + n].start()
    for n in range(chunks):
        loads[2 * chunks + n].start()
    gain_load = pltpu.make_async_copy(gain_hbm, gain, gain_sem)
    gain_load.start()

    def head(h):
        return pl.ds(h * DH, DH)

    later = lax.broadcasted_iota(jnp.int32, (rows, rows), 0) >= lax.broadcasted_iota(jnp.int32, (rows, rows), 1)

    def local_attention(h):
        cut = pl.ds(pl.multiple_of(h * DH, DH), DH)
        for r in range(2):
            part = pl.ds(r * rows, rows)
            qr = qb[part, cut]
            own_scores = lax.dot_general(qr, kb[part, cut], (((1,), (1,)), ((), ())), preferred_element_type=jnp.float32)
            weights = jnp.where(later, own_scores, 0.0).astype(jnp.bfloat16)
            acc = jnp.dot(weights, vb[part, cut], preferred_element_type=jnp.float32)
            if r == 1:
                top = pl.ds(0, rows)
                full = lax.dot_general(qr, kb[top, cut], (((1,), (1,)), ((), ())), preferred_element_type=jnp.float32)
                acc = acc + jnp.dot(full.astype(jnp.bfloat16), vb[top, cut], preferred_element_type=jnp.float32)
            mixed[part, cut] = acc

    heads_here = chunks * HPC

    def attend(start=0, stop=heads_here):
        @pl.loop(start, stop)
        def _(h):
            local_attention(h)

    def fill(part):
        @pl.when(jnp.logical_not(late))
        def _():
            attend(heads_here * FILL[part] // 6, heads_here * FILL[part + 1] // 6)

    def exchange(n):
        remote(kv.at[n], pk.at[n], sc.at[n], rc.at[n], partner)

    def make(n):
        loads[n].wait()
        loads[chunks + n].wait()
        cut = pl.ds(n * HPC * DH, HPC * DH)
        sums = lax.dot_general(kb[:, cut], vb[:, cut], (((0,), (0,)), ((), ())), preferred_element_type=jnp.float32)
        for j in range(HPC):
            kv[n, pl.ds(j * DH, DH), :] = sums[j * DH:(j + 1) * DH, j * DH:(j + 1) * DH]

    waits = jnp.logical_and(late, jnp.logical_not(first))

    @pl.when(waits)
    def _():
        for n in range(chunks):
            make(n)
        for load in loads[2 * chunks:]:
            load.wait()
        attend()
        greeted()
        for n in range(chunks):
            exchange(n)

    @pl.when(jnp.logical_not(waits))
    def _():
        for n in range(chunks):
            if n == 0:
                @pl.when(first)
                def _():
                    greeted()

            make(n)
            if n == 0:
                @pl.when(jnp.logical_not(first))
                def _():
                    greeted()

            @pl.when(first)
            def _():
                for i in range(nx):
                    remote(kv.at[n, pl.ds(half + i * slc, slc)], lk.at[n], sk.at[n, i], rk.at[n], {"seq": 2 * i + 1})

            exchange(n)
        for load in loads[2 * chunks:]:
            load.wait()

    gain_load.wait()
    def arrives(d):
        return jnp.logical_and(place >= d, z - d >= origin)

    for i, full in (*((d - 1, arrives(d)) for d in range(1, REACH)), (REACH - 1, z >= REACH)):
        @pl.when(jnp.logical_not(full))
        def _():
            for n in range(chunks):
                rw[n, i] = jnp.zeros((slc, DH), jnp.float32)

    mine = pl.ds(core * half, half)
    for n in range(chunks):
        @pl.when(mate)
        def _():
            ts[n] = kv[n, mine, :]

        @pl.when(jnp.logical_not(mate))
        def _():
            take(rc.at[n], pk.at[n])
            ts[n] = kv[n, mine, :] + pk[n, mine, :]

        for dx in (2, 1, 3):
            to = lax.rem(x + dx, nx)

            @pl.when(jnp.logical_not(jnp.logical_and(row, to == 0)))
            def _():
                remote(ts.at[n, pl.ds(to * slc, slc)], ra.at[n, pl.ds(x * slc, slc)], sa.at[n], rcv_a.at[n], chip(dx))

        ra[n, pl.ds(x * slc, slc), :] = ts[n, pl.ds(x * slc, slc), :]

    @pl.when(row)
    def _():
        pl.semaphore_wait(enter, 1)
        for n in range(chunks):
            remote(ts.at[n, pl.ds(0, slc)], ra.at[n, pl.ds(x * slc, slc)], sa.at[n], rcv_a.at[n], {"seq": 0})

    fill(0)

    for n in range(chunks):
        take(rcv_a.at[n], ra.at[n, pl.ds(0, (nx - 1) * slc)])

        @pl.when(jnp.logical_and(late, core == 1))
        def _():
            take(rk.at[n], lk.at[n])
            ra[n, pl.ds(0, slc), :] = ra[n, pl.ds(0, slc), :] + lk[n]

        total = ra[n, pl.ds(0, slc), :]
        for i in range(1, nx):
            total = total + ra[n, pl.ds(i * slc, slc), :]
        gs[n] = total
        for d in range(1, REACH):
            if n == 0:
                learn(d, place + d < REACH)

            @pl.when(inside(d))
            def _():
                remote(gs.at[n], rw.at[n, d - 1], s1.at[n, d - 1], r1.at[n, d - 1], {"grp": z + d})

        @pl.when(late)
        def _():
            if n == 0:
                pl.semaphore_wait(word, 1)
            for i, to in enumerate((1, 2, relay, *range(3, relay), end)):
                remote(gs.at[n], lt.at[n], sl.at[n, i], rl.at[n], {"grp": to})


    def pass_on(n, source, targets):
        @pl.when(z == source)
        def _():
            for i, to in enumerate(targets):
                remote(lt.at[n], lt.at[n], sl.at[n, i], rl.at[n], {"grp": to})

    @pl.when(final)
    def _():
        for n in range(chunks):
            take(rl.at[n], lt.at[n])
            pass_on(n, *fans[-1])

    fill(1)


    def hand_back(n, before):
        for i in range(nx):
            cs[n, pl.ds(i * slc, slc), :] = before
            before = before + ra[n, pl.ds(i * slc, slc), :]
        land = pl.ds(core * half + x * slc, slc)
        for dx in (2, 1, 3):
            to = lax.rem(x + dx, nx)
            remote(cs.at[n, pl.ds(to * slc, slc)], rf.at[n, land], s3.at[n], r3.at[n], chip(dx))
        rf[n, land, :] = cs[n, pl.ds(x * slc, slc), :]

    for n in range(chunks):
        for d in range(1, REACH):
            @pl.when(arrives(d))
            def _():
                take(r1.at[n, d - 1], rw.at[n, d - 1])

        near = rw[n, 0] + rw[n, 1] + rw[n, 2]

        @pl.when(z >= REACH)
        def _():
            take(r1.at[n, REACH - 1], rw.at[n, REACH - 1])

        before = rw[n, REACH - 1] + near
        run[n] = before + gs[n]
        for d in (REACH, *range(1, REACH)):
            if n == 0:
                learn(d, tail)

            @pl.when(jnp.logical_and(feeds(d), tail))
            def _():
                remote(run.at[n], rw.at[n, REACH - 1], s1.at[n, d - 1], r1.at[n, REACH - 1], {"grp": z + d})

        bf[n] = before

        @pl.when(jnp.logical_not(plane))
        def _():
            hand_back(n, bf[n])

    for d in range(1, REACH + 1):
        learn(d, jnp.logical_and(place + d >= REACH, jnp.logical_not(tail)))

    @pl.when(plane)
    def _():
        for n in range(chunks):
            @pl.when(jnp.logical_and(z >= 1, z < end))
            def _():
                take(rl.at[n], lt.at[n])
                for source, targets in fans[:-1]:
                    pass_on(n, source, targets)

            @pl.when(z >= 1)
            def _():
                bf[n] = bf[n] + lt[n]

            hand_back(n, bf[n])

    fill(2)
    for n in range(chunks):
        take(r3.at[n], rf.at[n, pl.ds(0, (nx - 1) * slc)])
        remote(rf.at[n, mine], rf.at[n, mine], s4.at[n], r4.at[n], partner)

    @pl.when(first)
    def _():
        attend()

    @pl.when(mate)
    def _():
        for n in range(chunks):
            take(rc.at[n], pk.at[n])

    second = core == 1
    for n in range(chunks):
        take(r4.at[n], rf.at[n, pl.ds(0, half)])
        for j in range(HPC):
            h = n * HPC + j
            at = pl.ds(j * DH, DH)
            state = rf[n, at, :] + jnp.where(second, pk[n, at, :], 0.0)
            m = mixed[:, head(h)] + jnp.dot(
                qb[:, head(h)], state.astype(jnp.bfloat16), preferred_element_type=jnp.float32
            )
            meansq = jnp.mean(m * m, axis=-1, keepdims=True)
            out_ref[:, head(h)] = (m * lax.rsqrt(meansq + eps) * gain[head(h)].reshape(1, DH)).astype(jnp.bfloat16)

    for n in range(chunks):
        take(sc.at[n], kv.at[n])
        take(sa.at[n], ts.at[n, pl.ds(0, (nx - 1) * slc)])
        take(s3.at[n], cs.at[n, pl.ds(0, (nx - 1) * slc)])
        take(s4.at[n], rf.at[n, pl.ds(0, half)])

        for d in range(1, REACH + 1):
            @pl.when(jnp.logical_and(feeds(d), jnp.logical_or(tail, place + d < REACH)))
            def _():
                take(s1.at[n, d - 1], gs.at[n])

        @pl.when(first)
        def _():
            for i in range(nx):
                take(sk.at[n, i], lk.at[n])

        @pl.when(late)
        def _():
            for i in range(relay + 1):
                take(sl.at[n, i], lt.at[n])

        for source, targets in fans:
            @pl.when(jnp.logical_and(plane, z == source))
            def _():
                for i in range(len(targets)):
                    take(sl.at[n, i], lt.at[n])


def per_device(query_feat, key_feat, value_feat, norm_gain):
    tokens, width = query_feat.shape[2:]
    nx, nz = lax.axis_size("seq") // 2, lax.axis_size("grp")
    chunks = width // (HPC * DH)
    half = HPC * DH // 2
    slc = half // nx
    f32 = jnp.float32
    dma = pltpu.SemaphoreType.DMA

    def kernel(*refs):
        body(nx, nz, 1e-05, *refs)

    hbm = pl.BlockSpec(memory_space=pltpu.HBM)
    vmem = pl.BlockSpec(memory_space=pltpu.VMEM)
    out = pl.pallas_call(
        kernel,
        out_shape=jax.ShapeDtypeStruct((tokens, width), jnp.bfloat16),
        in_specs=[hbm, hbm, hbm, hbm],
        out_specs=vmem,
        scratch_shapes=[
            pltpu.VMEM((tokens, width), jnp.bfloat16),
            pltpu.VMEM((tokens, width), jnp.bfloat16),
            pltpu.VMEM((tokens, width), jnp.bfloat16),
            pltpu.VMEM((width,), f32),
            pltpu.VMEM((tokens, width), f32),
            pltpu.VMEM((chunks, HPC * DH, DH), f32),
            pltpu.VMEM((chunks, HPC * DH, DH), f32),
            pltpu.VMEM((chunks, half, DH), f32),
            pltpu.VMEM((chunks, half, DH), f32),
            pltpu.VMEM((chunks, slc, DH), f32),
            pltpu.VMEM((chunks, REACH, slc, DH), f32),
            pltpu.VMEM((chunks, slc, DH), f32),
            pltpu.VMEM((chunks, slc, DH), f32),
            pltpu.VMEM((chunks, slc, DH), f32),
            pltpu.VMEM((chunks, slc, DH), f32),
            pltpu.VMEM((chunks, half, DH), f32),
            pltpu.VMEM((chunks, HPC * DH, DH), f32),
            dma((3, chunks)), dma,
            dma((chunks,)), dma((chunks,)),
            dma((chunks,)), dma((chunks,)),
            dma((chunks, REACH)), dma((chunks, REACH)),
            dma((chunks,)), dma((chunks,)),
            dma((chunks,)), dma((chunks,)),
            dma((chunks, nz)), dma((chunks,)),
            dma((chunks, nx)), dma((chunks,)),
            pltpu.SemaphoreType.REGULAR((REACH,)),
            pltpu.SemaphoreType.REGULAR,
            pltpu.SemaphoreType.REGULAR,
        ],
        compiler_params=pltpu.CompilerParams(collective_id=0, has_side_effects=True, vmem_limit_bytes=48 * 1024 * 1024),
        name="prefix_attention",
    )(
        *(
            pltpu.with_memory_space_constraint(a, pltpu.HBM)
            for a in (
                query_feat.reshape(tokens, width),
                key_feat.reshape(tokens, width),
                value_feat.reshape(tokens, width),
                norm_gain,
            )
        )
    )
    return out.reshape(query_feat.shape)


def solution(mesh):
    placed = (
        P("grp", "seq", None, "head"),
        P("grp", "seq", None, "head"),
        P("grp", "seq", None, "head"),
        P("head"),
    )
    return jax.shard_map(
        per_device,
        mesh=mesh,
        in_specs=placed,
        out_specs=P("grp", "seq", None, "head"),
        check_vma=False,
    )
```

```python
import jax
import jax.numpy as jnp
from jax import lax
from jax.experimental import pallas as pl
from jax.experimental.pallas import tpu as pltpu
from jax.sharding import PartitionSpec as P

DH = 128
MESH = pl.DeviceIdType.MESH
HPC = 3
REACH = 4
FILL = (0, 2, 4, 6)


def take(sem, ref):
    pltpu.make_async_copy(ref, ref, sem).wait()


def body(nx, nz, eps, q_hbm, k_hbm, v_hbm, gain_hbm, out_ref, qb, kb, vb, gain, mixed,
         kv, pk, ts, ra, gs, rw, run, bf, lt, lk, cs, rf,
         in_sem, gain_sem, sc, rc, sa, rcv_a, s1, r1, s3, r3, s4, r4, sl, rl, sk, rk, hello, word, enter):
    seq, z = lax.axis_index("seq"), lax.axis_index("grp")
    core, x = lax.rem(seq, 2), seq // 2
    tokens, width = qb.shape
    chunks = width // (HPC * DH)
    half = HPC * DH // 2
    slc = half // nx
    rows = tokens // 2
    plane = lax.axis_index("head") == 0
    late = jnp.logical_and(plane, z == 0)
    first = jnp.logical_and(late, seq == 0)
    mate = jnp.logical_and(late, seq == 1)
    others = jnp.logical_and(late, seq > 1)
    row, odd = jnp.logical_and(others, core == 0), jnp.logical_and(others, core == 1)
    origin = jnp.where(plane, 1, 0)
    relay, end = REACH, nz - 1
    final = jnp.logical_and(plane, z == end)

    middle = 2 * relay
    split = middle + 3
    fans = ((relay, (middle, *range(relay + 1, middle))), (middle, range(middle + 1, split)), (end, range(split, end)))

    place = lax.rem(z, REACH)
    tail = place == REACH - 1

    def inside(d):
        return jnp.logical_and(feeds(d), place + d < REACH)

    def feeds(d):
        return jnp.logical_and(z >= origin, z + d < nz)

    def chip(dx):
        return {"seq": lax.rem(x + dx, nx) * 2 + core}

    partner = {"seq": x * 2 + 1 - core}

    def remote(src, dst, send, recv, where):
        pltpu.make_async_remote_copy(
            src_ref=src, dst_ref=dst, send_sem=send, recv_sem=recv, device_id=where, device_id_type=MESH
        ).start()

    loads = []
    for i, (hbm, buf) in enumerate(((k_hbm, kb), (v_hbm, vb), (q_hbm, qb))):
        for n in range(chunks):
            cols = pl.ds(n * HPC * DH, HPC * DH)
            loads.append(pltpu.make_async_copy(hbm.at[:, cols], buf.at[:, cols], in_sem.at[i, n]))
    for n in range(chunks):
        loads[n].start()
        loads[chunks + n].start()
    for n in range(chunks):
        loads[2 * chunks + n].start()
    gain_load = pltpu.make_async_copy(gain_hbm, gain, gain_sem)
    gain_load.start()

    barrier = pltpu.get_barrier_semaphore()
    pl.semaphore_signal(barrier, inc=1, device_id=partner, device_id_type=MESH)

    @pl.when(jnp.logical_not(first))
    def _():
        for dx in range(1, nx):
            pl.semaphore_signal(barrier, inc=1, device_id=chip(dx), device_id_type=MESH)

    notes = [(feeds(d), z + d) for d in range(1, REACH + 1)]
    @pl.when(odd)
    def _():
        pl.semaphore_signal(barrier, inc=1, device_id={"seq": 0}, device_id_type=MESH)

    notes += [(jnp.logical_and(plane, jnp.logical_and(z >= 1, z <= relay)), 0), (late, end)]
    for there, to in notes:
        @pl.when(there)
        def _():
            pl.semaphore_signal(barrier, inc=1, device_id={"grp": to}, device_id_type=MESH)

    def greeted():
        behind = jnp.minimum(jnp.maximum(z - origin, 0), REACH)
        behind = behind + jnp.where(first, nx - 1, 0) - jnp.where(row, 1, 0)
        pl.semaphore_wait(barrier, nx + behind + jnp.where(late, relay, 0) + jnp.where(final, 1, 0))
        for d in range(1, REACH + 1):
            @pl.when(z - d >= origin)
            def _():
                pl.semaphore_signal(hello.at[d - 1], inc=1, device_id={"grp": z - d}, device_id_type=MESH)

        @pl.when(final)
        def _():
            pl.semaphore_signal(word, inc=1, device_id={"grp": 0}, device_id_type=MESH)

        @pl.when(first)
        def _():
            for i in range(1, nx):
                pl.semaphore_signal(enter, inc=1, device_id={"seq": 2 * i}, device_id_type=MESH)

    def learn(d, wanted):
        @pl.when(jnp.logical_and(feeds(d), wanted))
        def _():
            pl.semaphore_wait(hello.at[d - 1], 1)

    def head(h):
        return pl.ds(h * DH, DH)

    later = lax.broadcasted_iota(jnp.int32, (rows, rows), 0) >= lax.broadcasted_iota(jnp.int32, (rows, rows), 1)

    def local_attention(h):
        cut = pl.ds(pl.multiple_of(h * DH, DH), DH)
        for r in range(2):
            part = pl.ds(r * rows, rows)
            qr = qb[part, cut]
            own_scores = lax.dot_general(qr, kb[part, cut], (((1,), (1,)), ((), ())), preferred_element_type=jnp.float32)
            weights = jnp.where(later, own_scores, 0.0).astype(jnp.bfloat16)
            acc = jnp.dot(weights, vb[part, cut], preferred_element_type=jnp.float32)
            if r == 1:
                top = pl.ds(0, rows)
                full = lax.dot_general(qr, kb[top, cut], (((1,), (1,)), ((), ())), preferred_element_type=jnp.float32)
                acc = acc + jnp.dot(full.astype(jnp.bfloat16), vb[top, cut], preferred_element_type=jnp.float32)
            mixed[part, cut] = acc

    heads_here = chunks * HPC

    def attend(start=0, stop=heads_here):
        @pl.loop(start, stop)
        def _(h):
            local_attention(h)

    def fill(part):
        @pl.when(jnp.logical_not(late))
        def _():
            attend(heads_here * FILL[part] // 6, heads_here * FILL[part + 1] // 6)

    def exchange(n):
        remote(kv.at[n], pk.at[n], sc.at[n], rc.at[n], partner)

    def make(n):
        loads[n].wait()
        loads[chunks + n].wait()
        cut = pl.ds(n * HPC * DH, HPC * DH)
        sums = lax.dot_general(kb[:, cut], vb[:, cut], (((0,), (0,)), ((), ())), preferred_element_type=jnp.float32)
        for j in range(HPC):
            kv[n, pl.ds(j * DH, DH), :] = sums[j * DH:(j + 1) * DH, j * DH:(j + 1) * DH]

    waits = jnp.logical_and(late, jnp.logical_not(first))

    @pl.when(waits)
    def _():
        for n in range(chunks):
            make(n)
        for load in loads[2 * chunks:]:
            load.wait()
        attend()
        greeted()
        for n in range(chunks):
            exchange(n)

    @pl.when(jnp.logical_not(waits))
    def _():
        for n in range(chunks):
            if n == 0:
                @pl.when(first)
                def _():
                    greeted()

            make(n)
            if n == 0:
                @pl.when(jnp.logical_not(first))
                def _():
                    greeted()

            @pl.when(first)
            def _():
                for i in range(nx):
                    remote(kv.at[n, pl.ds(half + i * slc, slc)], lk.at[n], sk.at[n, i], rk.at[n], {"seq": 2 * i + 1})

            exchange(n)
        for load in loads[2 * chunks:]:
            load.wait()

    gain_load.wait()
    def arrives(d):
        return jnp.logical_and(place >= d, z - d >= origin)

    for i, full in (*((d - 1, arrives(d)) for d in range(1, REACH)), (REACH - 1, z >= REACH)):
        @pl.when(jnp.logical_not(full))
        def _():
            for n in range(chunks):
                rw[n, i] = jnp.zeros((slc, DH), jnp.float32)

    mine = pl.ds(core * half, half)
    for n in range(chunks):
        @pl.when(mate)
        def _():
            ts[n] = kv[n, mine, :]

        @pl.when(jnp.logical_not(mate))
        def _():
            take(rc.at[n], pk.at[n])
            ts[n] = kv[n, mine, :] + pk[n, mine, :]

        for dx in (2, 1, 3):
            to = lax.rem(x + dx, nx)

            @pl.when(jnp.logical_not(jnp.logical_and(row, to == 0)))
            def _():
                remote(ts.at[n, pl.ds(to * slc, slc)], ra.at[n, pl.ds(x * slc, slc)], sa.at[n], rcv_a.at[n], chip(dx))

        ra[n, pl.ds(x * slc, slc), :] = ts[n, pl.ds(x * slc, slc), :]

    @pl.when(row)
    def _():
        pl.semaphore_wait(enter, 1)
        for n in range(chunks):
            remote(ts.at[n, pl.ds(0, slc)], ra.at[n, pl.ds(x * slc, slc)], sa.at[n], rcv_a.at[n], {"seq": 0})

    fill(0)

    for n in range(chunks):
        take(rcv_a.at[n], ra.at[n, pl.ds(0, (nx - 1) * slc)])

        @pl.when(jnp.logical_and(late, core == 1))
        def _():
            take(rk.at[n], lk.at[n])
            ra[n, pl.ds(0, slc), :] = ra[n, pl.ds(0, slc), :] + lk[n]

        total = ra[n, pl.ds(0, slc), :]
        for i in range(1, nx):
            total = total + ra[n, pl.ds(i * slc, slc), :]
        gs[n] = total
        for d in range(1, REACH):
            if n == 0:
                learn(d, place + d < REACH)

            @pl.when(inside(d))
            def _():
                remote(gs.at[n], rw.at[n, d - 1], s1.at[n, d - 1], r1.at[n, d - 1], {"grp": z + d})

        @pl.when(late)
        def _():
            for i, to in enumerate((1, 2, relay)):
                remote(gs.at[n], lt.at[n], sl.at[n, i], rl.at[n], {"grp": to})


    @pl.when(late)
    def _():
        pl.semaphore_wait(word, 1)
        for n in range(chunks):
            for i, to in enumerate((*range(3, relay), end)):
                remote(gs.at[n], lt.at[n], sl.at[n, 3 + i], rl.at[n], {"grp": to})

    def pass_on(n, source, targets):
        @pl.when(z == source)
        def _():
            for i, to in enumerate(targets):
                remote(lt.at[n], lt.at[n], sl.at[n, i], rl.at[n], {"grp": to})

    @pl.when(final)
    def _():
        for n in range(chunks):
            take(rl.at[n], lt.at[n])
            pass_on(n, *fans[-1])

    fill(1)


    def hand_back(n, before):
        for i in range(nx):
            cs[n, pl.ds(i * slc, slc), :] = before
            before = before + ra[n, pl.ds(i * slc, slc), :]
        land = pl.ds(core * half + x * slc, slc)
        for dx in (2, 1, 3):
            to = lax.rem(x + dx, nx)
            remote(cs.at[n, pl.ds(to * slc, slc)], rf.at[n, land], s3.at[n], r3.at[n], chip(dx))
        rf[n, land, :] = cs[n, pl.ds(x * slc, slc), :]

    for n in range(chunks):
        for d in range(1, REACH):
            @pl.when(arrives(d))
            def _():
                take(r1.at[n, d - 1], rw.at[n, d - 1])

        near = rw[n, 0] + rw[n, 1] + rw[n, 2]

        @pl.when(z >= REACH)
        def _():
            take(r1.at[n, REACH - 1], rw.at[n, REACH - 1])

        before = rw[n, REACH - 1] + near
        run[n] = before + gs[n]
        for d in (REACH, *range(1, REACH)):
            if n == 0:
                learn(d, tail)

            @pl.when(jnp.logical_and(feeds(d), tail))
            def _():
                remote(run.at[n], rw.at[n, REACH - 1], s1.at[n, d - 1], r1.at[n, REACH - 1], {"grp": z + d})

        bf[n] = before

        @pl.when(jnp.logical_not(plane))
        def _():
            hand_back(n, bf[n])

    for d in range(1, REACH + 1):
        learn(d, jnp.logical_and(place + d >= REACH, jnp.logical_not(tail)))

    @pl.when(plane)
    def _():
        for n in range(chunks):
            @pl.when(jnp.logical_and(z >= 1, z < end))
            def _():
                take(rl.at[n], lt.at[n])
                for source, targets in fans[:-1]:
                    pass_on(n, source, targets)

            @pl.when(z >= 1)
            def _():
                bf[n] = bf[n] + lt[n]

            hand_back(n, bf[n])

    fill(2)
    for n in range(chunks):
        take(r3.at[n], rf.at[n, pl.ds(0, (nx - 1) * slc)])
        remote(rf.at[n, mine], rf.at[n, mine], s4.at[n], r4.at[n], partner)

    @pl.when(first)
    def _():
        attend()

    @pl.when(mate)
    def _():
        for n in range(chunks):
            take(rc.at[n], pk.at[n])

    for n in range(chunks):
        take(sc.at[n], kv.at[n])
        take(sa.at[n], ts.at[n, pl.ds(0, (nx - 1) * slc)])
        take(s3.at[n], cs.at[n, pl.ds(0, (nx - 1) * slc)])

        for d in range(1, REACH + 1):
            @pl.when(jnp.logical_and(feeds(d), jnp.logical_or(tail, place + d < REACH)))
            def _():
                take(s1.at[n, d - 1], gs.at[n])

        @pl.when(first)
        def _():
            for i in range(nx):
                take(sk.at[n, i], lk.at[n])

        @pl.when(late)
        def _():
            for i in range(relay + 1):
                take(sl.at[n, i], lt.at[n])

        for source, targets in fans:
            @pl.when(jnp.logical_and(plane, z == source))
            def _():
                for i in range(len(targets)):
                    take(sl.at[n, i], lt.at[n])

    second = core == 1
    for n in range(chunks):
        take(r4.at[n], rf.at[n, pl.ds(0, half)])
        for j in range(HPC):
            h = n * HPC + j
            at = pl.ds(j * DH, DH)
            state = rf[n, at, :] + jnp.where(second, pk[n, at, :], 0.0)
            m = mixed[:, head(h)] + jnp.dot(
                qb[:, head(h)], state.astype(jnp.bfloat16), preferred_element_type=jnp.float32
            )
            meansq = jnp.mean(m * m, axis=-1, keepdims=True)
            out_ref[:, head(h)] = (m * lax.rsqrt(meansq + eps) * gain[head(h)].reshape(1, DH)).astype(jnp.bfloat16)

    for n in range(chunks):
        take(s4.at[n], rf.at[n, pl.ds(0, half)])


def per_device(query_feat, key_feat, value_feat, norm_gain):
    tokens, width = query_feat.shape[2:]
    nx, nz = lax.axis_size("seq") // 2, lax.axis_size("grp")
    chunks = width // (HPC * DH)
    half = HPC * DH // 2
    slc = half // nx
    f32 = jnp.float32
    dma = pltpu.SemaphoreType.DMA

    def kernel(*refs):
        body(nx, nz, 1e-05, *refs)

    hbm = pl.BlockSpec(memory_space=pltpu.HBM)
    vmem = pl.BlockSpec(memory_space=pltpu.VMEM)
    out = pl.pallas_call(
        kernel,
        out_shape=jax.ShapeDtypeStruct((tokens, width), jnp.bfloat16),
        in_specs=[hbm, hbm, hbm, hbm],
        out_specs=vmem,
        scratch_shapes=[
            pltpu.VMEM((tokens, width), jnp.bfloat16),
            pltpu.VMEM((tokens, width), jnp.bfloat16),
            pltpu.VMEM((tokens, width), jnp.bfloat16),
            pltpu.VMEM((width,), f32),
            pltpu.VMEM((tokens, width), f32),
            pltpu.VMEM((chunks, HPC * DH, DH), f32),
            pltpu.VMEM((chunks, HPC * DH, DH), f32),
            pltpu.VMEM((chunks, half, DH), f32),
            pltpu.VMEM((chunks, half, DH), f32),
            pltpu.VMEM((chunks, slc, DH), f32),
            pltpu.VMEM((chunks, REACH, slc, DH), f32),
            pltpu.VMEM((chunks, slc, DH), f32),
            pltpu.VMEM((chunks, slc, DH), f32),
            pltpu.VMEM((chunks, slc, DH), f32),
            pltpu.VMEM((chunks, slc, DH), f32),
            pltpu.VMEM((chunks, half, DH), f32),
            pltpu.VMEM((chunks, HPC * DH, DH), f32),
            dma((3, chunks)), dma,
            dma((chunks,)), dma((chunks,)),
            dma((chunks,)), dma((chunks,)),
            dma((chunks, REACH)), dma((chunks, REACH)),
            dma((chunks,)), dma((chunks,)),
            dma((chunks,)), dma((chunks,)),
            dma((chunks, nz)), dma((chunks,)),
            dma((chunks, nx)), dma((chunks,)),
            pltpu.SemaphoreType.REGULAR((REACH,)),
            pltpu.SemaphoreType.REGULAR,
            pltpu.SemaphoreType.REGULAR,
        ],
        compiler_params=pltpu.CompilerParams(collective_id=0, has_side_effects=True, vmem_limit_bytes=48 * 1024 * 1024),
        name="prefix_attention",
    )(
        *(
            pltpu.with_memory_space_constraint(a, pltpu.HBM)
            for a in (
                query_feat.reshape(tokens, width),
                key_feat.reshape(tokens, width),
                value_feat.reshape(tokens, width),
                norm_gain,
            )
        )
    )
    return out.reshape(query_feat.shape)


def solution(mesh):
    placed = (
        P("grp", "seq", None, "head"),
        P("grp", "seq", None, "head"),
        P("grp", "seq", None, "head"),
        P("head"),
    )
    return jax.shard_map(
        per_device,
        mesh=mesh,
        in_specs=placed,
        out_specs=P("grp", "seq", None, "head"),
        check_vma=False,
    )
```

```python
import jax
import jax.numpy as jnp
from jax import lax
from jax.experimental import pallas as pl
from jax.experimental.pallas import tpu as pltpu
from jax.sharding import PartitionSpec as P

DH = 128
MESH = pl.DeviceIdType.MESH
HPC = 3
REACH = 4
FILL = (0, 2, 4, 6)


def take(sem, ref):
    pltpu.make_async_copy(ref, ref, sem).wait()


def body(nx, nz, eps, q_hbm, k_hbm, v_hbm, gain_hbm, out_ref, qb, kb, vb, gain, mixed,
         kv, pk, ts, ra, gs, rw, run, bf, lt, lk, cs, rf,
         in_sem, gain_sem, sc, rc, sa, rcv_a, s1, r1, s3, r3, s4, r4, sl, rl, sk, rk, hello, word, enter):
    seq, z = lax.axis_index("seq"), lax.axis_index("grp")
    core, x = lax.rem(seq, 2), seq // 2
    tokens, width = qb.shape
    chunks = width // (HPC * DH)
    half = HPC * DH // 2
    slc = half // nx
    rows = tokens // 2
    plane = lax.axis_index("head") == 0
    late = jnp.logical_and(plane, z == 0)
    first = jnp.logical_and(late, seq == 0)
    mate = jnp.logical_and(late, seq == 1)
    others = jnp.logical_and(late, seq > 1)
    row, odd = jnp.logical_and(others, core == 0), jnp.logical_and(others, core == 1)
    origin = jnp.where(plane, 1, 0)
    relay, end = REACH, nz - 1
    final = jnp.logical_and(plane, z == end)

    middle = 2 * relay
    split = middle + 3
    fans = ((relay, (middle, *range(relay + 1, middle))), (middle, range(middle + 1, split)), (end, range(split, end)))

    place = lax.rem(z, REACH)
    tail = place == REACH - 1

    def inside(d):
        return jnp.logical_and(feeds(d), place + d < REACH)

    def feeds(d):
        return jnp.logical_and(z >= origin, z + d < nz)

    def chip(dx):
        return {"seq": lax.rem(x + dx, nx) * 2 + core}

    partner = {"seq": x * 2 + 1 - core}

    def remote(src, dst, send, recv, where):
        pltpu.make_async_remote_copy(
            src_ref=src, dst_ref=dst, send_sem=send, recv_sem=recv, device_id=where, device_id_type=MESH
        ).start()

    loads = []
    for i, (hbm, buf) in enumerate(((k_hbm, kb), (v_hbm, vb), (q_hbm, qb))):
        for n in range(chunks):
            cols = pl.ds(n * HPC * DH, HPC * DH)
            loads.append(pltpu.make_async_copy(hbm.at[:, cols], buf.at[:, cols], in_sem.at[i, n]))
    for n in range(chunks):
        loads[n].start()
        loads[chunks + n].start()
    for n in range(chunks):
        loads[2 * chunks + n].start()
    gain_load = pltpu.make_async_copy(gain_hbm, gain, gain_sem)
    gain_load.start()

    barrier = pltpu.get_barrier_semaphore()
    pl.semaphore_signal(barrier, inc=1, device_id=partner, device_id_type=MESH)

    @pl.when(jnp.logical_not(first))
    def _():
        for dx in range(1, nx):
            pl.semaphore_signal(barrier, inc=1, device_id=chip(dx), device_id_type=MESH)

    notes = [(feeds(d), z + d) for d in range(1, REACH + 1)]
    @pl.when(odd)
    def _():
        pl.semaphore_signal(barrier, inc=1, device_id={"seq": 0}, device_id_type=MESH)

    notes += [(jnp.logical_and(plane, jnp.logical_and(z >= 1, z <= relay)), 0), (late, end)]
    for there, to in notes:
        @pl.when(there)
        def _():
            pl.semaphore_signal(barrier, inc=1, device_id={"grp": to}, device_id_type=MESH)

    def greeted():
        behind = jnp.minimum(jnp.maximum(z - origin, 0), REACH)
        behind = behind + jnp.where(first, nx - 1, 0) - jnp.where(row, 1, 0)
        pl.semaphore_wait(barrier, nx + behind + jnp.where(late, relay, 0) + jnp.where(final, 1, 0))
        for d in range(1, REACH + 1):
            @pl.when(z - d >= origin)
            def _():
                pl.semaphore_signal(hello.at[d - 1], inc=1, device_id={"grp": z - d}, device_id_type=MESH)

        @pl.when(final)
        def _():
            pl.semaphore_signal(word, inc=1, device_id={"grp": 0}, device_id_type=MESH)

        @pl.when(first)
        def _():
            for i in range(1, nx):
                pl.semaphore_signal(enter, inc=1, device_id={"seq": 2 * i}, device_id_type=MESH)

    def learn(d, wanted):
        @pl.when(jnp.logical_and(feeds(d), wanted))
        def _():
            pl.semaphore_wait(hello.at[d - 1], 1)

    def head(h):
        return pl.ds(h * DH, DH)

    later = lax.broadcasted_iota(jnp.int32, (rows, rows), 0) >= lax.broadcasted_iota(jnp.int32, (rows, rows), 1)

    def local_attention(h):
        cut = pl.ds(pl.multiple_of(h * DH, DH), DH)
        for r in range(2):
            part = pl.ds(r * rows, rows)
            qr = qb[part, cut]
            own_scores = lax.dot_general(qr, kb[part, cut], (((1,), (1,)), ((), ())), preferred_element_type=jnp.float32)
            weights = jnp.where(later, own_scores, 0.0).astype(jnp.bfloat16)
            acc = jnp.dot(weights, vb[part, cut], preferred_element_type=jnp.float32)
            if r == 1:
                top = pl.ds(0, rows)
                full = lax.dot_general(qr, kb[top, cut], (((1,), (1,)), ((), ())), preferred_element_type=jnp.float32)
                acc = acc + jnp.dot(full.astype(jnp.bfloat16), vb[top, cut], preferred_element_type=jnp.float32)
            mixed[part, cut] = acc

    heads_here = chunks * HPC

    def attend(start=0, stop=heads_here):
        @pl.loop(start, stop)
        def _(h):
            local_attention(h)

    def fill(part):
        @pl.when(jnp.logical_not(late))
        def _():
            attend(heads_here * FILL[part] // 6, heads_here * FILL[part + 1] // 6)

    def exchange(n):
        remote(kv.at[n], pk.at[n], sc.at[n], rc.at[n], partner)

    def make(n):
        loads[n].wait()
        loads[chunks + n].wait()
        for j in range(HPC):
            cut = head(n * HPC + j)
            kv[n, pl.ds(j * DH, DH), :] = lax.dot_general(
                kb[:, cut], vb[:, cut], (((0,), (0,)), ((), ())), preferred_element_type=jnp.float32
            )

    waits = jnp.logical_and(late, jnp.logical_not(first))

    @pl.when(waits)
    def _():
        for n in range(chunks):
            make(n)
        for load in loads[2 * chunks:]:
            load.wait()
        attend()
        greeted()
        for n in range(chunks):
            exchange(n)

    @pl.when(jnp.logical_not(waits))
    def _():
        for n in range(chunks):
            if n == 0:
                @pl.when(first)
                def _():
                    greeted()

            make(n)
            if n == 0:
                @pl.when(jnp.logical_not(first))
                def _():
                    greeted()

            @pl.when(first)
            def _():
                for i in range(nx):
                    remote(kv.at[n, pl.ds(half + i * slc, slc)], lk.at[n], sk.at[n, i], rk.at[n], {"seq": 2 * i + 1})

            exchange(n)
        for load in loads[2 * chunks:]:
            load.wait()

    gain_load.wait()
    def arrives(d):
        return jnp.logical_and(place >= d, z - d >= origin)

    for i, full in (*((d - 1, arrives(d)) for d in range(1, REACH)), (REACH - 1, z >= REACH)):
        @pl.when(jnp.logical_not(full))
        def _():
            for n in range(chunks):
                rw[n, i] = jnp.zeros((slc, DH), jnp.float32)

    mine = pl.ds(core * half, half)
    for n in range(chunks):
        @pl.when(mate)
        def _():
            ts[n] = kv[n, mine, :]

        @pl.when(jnp.logical_not(mate))
        def _():
            take(rc.at[n], pk.at[n])
            ts[n] = kv[n, mine, :] + pk[n, mine, :]

        for dx in (2, 1, 3):
            to = lax.rem(x + dx, nx)

            @pl.when(jnp.logical_not(jnp.logical_and(row, to == 0)))
            def _():
                remote(ts.at[n, pl.ds(to * slc, slc)], ra.at[n, pl.ds(x * slc, slc)], sa.at[n], rcv_a.at[n], chip(dx))

        ra[n, pl.ds(x * slc, slc), :] = ts[n, pl.ds(x * slc, slc), :]

    @pl.when(row)
    def _():
        pl.semaphore_wait(enter, 1)
        for n in range(chunks):
            remote(ts.at[n, pl.ds(0, slc)], ra.at[n, pl.ds(x * slc, slc)], sa.at[n], rcv_a.at[n], {"seq": 0})

    fill(0)

    for n in range(chunks):
        take(rcv_a.at[n], ra.at[n, pl.ds(0, (nx - 1) * slc)])

        @pl.when(jnp.logical_and(late, core == 1))
        def _():
            take(rk.at[n], lk.at[n])
            ra[n, pl.ds(0, slc), :] = ra[n, pl.ds(0, slc), :] + lk[n]

        total = ra[n, pl.ds(0, slc), :]
        for i in range(1, nx):
            total = total + ra[n, pl.ds(i * slc, slc), :]
        gs[n] = total
        for d in range(1, REACH):
            if n == 0:
                learn(d, place + d < REACH)

            @pl.when(inside(d))
            def _():
                remote(gs.at[n], rw.at[n, d - 1], s1.at[n, d - 1], r1.at[n, d - 1], {"grp": z + d})

        @pl.when(late)
        def _():
            for i, to in enumerate((1, 2, relay)):
                remote(gs.at[n], lt.at[n], sl.at[n, i], rl.at[n], {"grp": to})


    @pl.when(late)
    def _():
        pl.semaphore_wait(word, 1)
        for n in range(chunks):
            for i, to in enumerate((*range(3, relay), end)):
                remote(gs.at[n], lt.at[n], sl.at[n, 3 + i], rl.at[n], {"grp": to})

    def pass_on(n, source, targets):
        @pl.when(z == source)
        def _():
            for i, to in enumerate(targets):
                remote(lt.at[n], lt.at[n], sl.at[n, i], rl.at[n], {"grp": to})

    @pl.when(final)
    def _():
        for n in range(chunks):
            take(rl.at[n], lt.at[n])
            pass_on(n, *fans[-1])

    fill(1)


    def hand_back(n, before):
        for i in range(nx):
            cs[n, pl.ds(i * slc, slc), :] = before
            before = before + ra[n, pl.ds(i * slc, slc), :]
        land = pl.ds(core * half + x * slc, slc)
        for dx in (2, 1, 3):
            to = lax.rem(x + dx, nx)
            remote(cs.at[n, pl.ds(to * slc, slc)], rf.at[n, land], s3.at[n], r3.at[n], chip(dx))
        rf[n, land, :] = cs[n, pl.ds(x * slc, slc), :]

    for n in range(chunks):
        for d in range(1, REACH):
            @pl.when(arrives(d))
            def _():
                take(r1.at[n, d - 1], rw.at[n, d - 1])

        near = rw[n, 0] + rw[n, 1] + rw[n, 2]

        @pl.when(z >= REACH)
        def _():
            take(r1.at[n, REACH - 1], rw.at[n, REACH - 1])

        before = rw[n, REACH - 1] + near
        run[n] = before + gs[n]
        for d in (REACH, *range(1, REACH)):
            if n == 0:
                learn(d, tail)

            @pl.when(jnp.logical_and(feeds(d), tail))
            def _():
                remote(run.at[n], rw.at[n, REACH - 1], s1.at[n, d - 1], r1.at[n, REACH - 1], {"grp": z + d})

        bf[n] = before

        @pl.when(jnp.logical_not(plane))
        def _():
            hand_back(n, bf[n])

    for d in range(1, REACH + 1):
        learn(d, jnp.logical_and(place + d >= REACH, jnp.logical_not(tail)))

    @pl.when(plane)
    def _():
        for n in range(chunks):
            @pl.when(jnp.logical_and(z >= 1, z < end))
            def _():
                take(rl.at[n], lt.at[n])
                for source, targets in fans[:-1]:
                    pass_on(n, source, targets)

            @pl.when(z >= 1)
            def _():
                bf[n] = bf[n] + lt[n]

            hand_back(n, bf[n])

    fill(2)
    for n in range(chunks):
        take(r3.at[n], rf.at[n, pl.ds(0, (nx - 1) * slc)])
        remote(rf.at[n, mine], rf.at[n, mine], s4.at[n], r4.at[n], partner)

    @pl.when(first)
    def _():
        attend()

    @pl.when(mate)
    def _():
        for n in range(chunks):
            take(rc.at[n], pk.at[n])

    for n in range(chunks):
        take(sc.at[n], kv.at[n])
        take(sa.at[n], ts.at[n, pl.ds(0, (nx - 1) * slc)])
        take(s3.at[n], cs.at[n, pl.ds(0, (nx - 1) * slc)])

        for d in range(1, REACH + 1):
            @pl.when(jnp.logical_and(feeds(d), jnp.logical_or(tail, place + d < REACH)))
            def _():
                take(s1.at[n, d - 1], gs.at[n])

        @pl.when(first)
        def _():
            for i in range(nx):
                take(sk.at[n, i], lk.at[n])

        @pl.when(late)
        def _():
            for i in range(relay + 1):
                take(sl.at[n, i], lt.at[n])

        for source, targets in fans:
            @pl.when(jnp.logical_and(plane, z == source))
            def _():
                for i in range(len(targets)):
                    take(sl.at[n, i], lt.at[n])

    second = core == 1

    def finish(n, j):
        cut = pl.ds(pl.multiple_of((n * HPC + j) * DH, DH), DH)
        at = pl.ds(pl.multiple_of(j * DH, DH), DH)
        state = rf[n, at, :] + jnp.where(second, pk[n, at, :], 0.0)
        m = mixed[:, cut] + jnp.dot(qb[:, cut], state.astype(jnp.bfloat16), preferred_element_type=jnp.float32)
        meansq = jnp.mean(m * m, axis=-1, keepdims=True)
        scale = gain[head(n * HPC)]
        for i in range(1, HPC):
            scale = jnp.where(j == i, gain[head(n * HPC + i)], scale)
        out_ref[:, cut] = (m * lax.rsqrt(meansq + eps) * scale.reshape(1, DH)).astype(jnp.bfloat16)

    for n in range(chunks):
        finish(n, (HPC - 1) * core)
    for n in range(chunks):
        take(r4.at[n], rf.at[n, pl.ds(0, half)])
        for i in range(1, HPC - 1):
            finish(n, i)
        finish(n, (HPC - 1) * (1 - core))

    for n in range(chunks):
        take(s4.at[n], rf.at[n, pl.ds(0, half)])


def per_device(query_feat, key_feat, value_feat, norm_gain):
    tokens, width = query_feat.shape[2:]
    nx, nz = lax.axis_size("seq") // 2, lax.axis_size("grp")
    chunks = width // (HPC * DH)
    half = HPC * DH // 2
    slc = half // nx
    f32 = jnp.float32
    dma = pltpu.SemaphoreType.DMA

    def kernel(*refs):
        body(nx, nz, 1e-05, *refs)

    hbm = pl.BlockSpec(memory_space=pltpu.HBM)
    vmem = pl.BlockSpec(memory_space=pltpu.VMEM)
    out = pl.pallas_call(
        kernel,
        out_shape=jax.ShapeDtypeStruct((tokens, width), jnp.bfloat16),
        in_specs=[hbm, hbm, hbm, hbm],
        out_specs=vmem,
        scratch_shapes=[
            pltpu.VMEM((tokens, width), jnp.bfloat16),
            pltpu.VMEM((tokens, width), jnp.bfloat16),
            pltpu.VMEM((tokens, width), jnp.bfloat16),
            pltpu.VMEM((width,), f32),
            pltpu.VMEM((tokens, width), f32),
            pltpu.VMEM((chunks, HPC * DH, DH), f32),
            pltpu.VMEM((chunks, HPC * DH, DH), f32),
            pltpu.VMEM((chunks, half, DH), f32),
            pltpu.VMEM((chunks, half, DH), f32),
            pltpu.VMEM((chunks, slc, DH), f32),
            pltpu.VMEM((chunks, REACH, slc, DH), f32),
            pltpu.VMEM((chunks, slc, DH), f32),
            pltpu.VMEM((chunks, slc, DH), f32),
            pltpu.VMEM((chunks, slc, DH), f32),
            pltpu.VMEM((chunks, slc, DH), f32),
            pltpu.VMEM((chunks, half, DH), f32),
            pltpu.VMEM((chunks, HPC * DH, DH), f32),
            dma((3, chunks)), dma,
            dma((chunks,)), dma((chunks,)),
            dma((chunks,)), dma((chunks,)),
            dma((chunks, REACH)), dma((chunks, REACH)),
            dma((chunks,)), dma((chunks,)),
            dma((chunks,)), dma((chunks,)),
            dma((chunks, nz)), dma((chunks,)),
            dma((chunks, nx)), dma((chunks,)),
            pltpu.SemaphoreType.REGULAR((REACH,)),
            pltpu.SemaphoreType.REGULAR,
            pltpu.SemaphoreType.REGULAR,
        ],
        compiler_params=pltpu.CompilerParams(collective_id=0, has_side_effects=True, vmem_limit_bytes=48 * 1024 * 1024),
        name="prefix_attention",
    )(
        *(
            pltpu.with_memory_space_constraint(a, pltpu.HBM)
            for a in (
                query_feat.reshape(tokens, width),
                key_feat.reshape(tokens, width),
                value_feat.reshape(tokens, width),
                norm_gain,
            )
        )
    )
    return out.reshape(query_feat.shape)


def solution(mesh):
    placed = (
        P("grp", "seq", None, "head"),
        P("grp", "seq", None, "head"),
        P("grp", "seq", None, "head"),
        P("head"),
    )
    return jax.shard_map(
        per_device,
        mesh=mesh,
        in_specs=placed,
        out_specs=P("grp", "seq", None, "head"),
        check_vma=False,
    )
```

```python
import jax
import jax.numpy as jnp
from jax import lax
from jax.experimental import pallas as pl
from jax.experimental.pallas import tpu as pltpu
from jax.sharding import PartitionSpec as P

DH = 128
MESH = pl.DeviceIdType.MESH
HPC = 3
REACH = 4
FILL = (0, 2, 4, 6)


def take(sem, ref):
    pltpu.make_async_copy(ref, ref, sem).wait()


def body(nx, nz, eps, q_hbm, k_hbm, v_hbm, gain_hbm, out_ref, qb, kb, vb, gain, mixed,
         kv, pk, ts, ra, gs, rw, run, bf, lt, lk, cs, rf,
         in_sem, gain_sem, sc, rc, sa, rcv_a, s1, r1, s3, r3, s4, r4, sl, rl, sk, rk, hello, word, enter):
    seq, z = lax.axis_index("seq"), lax.axis_index("grp")
    core, x = lax.rem(seq, 2), seq // 2
    tokens, width = qb.shape
    chunks = width // (HPC * DH)
    half = HPC * DH // 2
    slc = half // nx
    rows = tokens // 2
    plane = lax.axis_index("head") == 0
    late = jnp.logical_and(plane, z == 0)
    first = jnp.logical_and(late, seq == 0)
    mate = jnp.logical_and(late, seq == 1)
    others = jnp.logical_and(late, seq > 1)
    row, odd = jnp.logical_and(others, core == 0), jnp.logical_and(others, core == 1)
    origin = jnp.where(plane, 1, 0)
    relay, end = REACH, nz - 1
    final = jnp.logical_and(plane, z == end)

    middle = 2 * relay
    split = middle + 3
    fans = ((relay, (middle, *range(relay + 1, middle))), (middle, range(middle + 1, split)), (end, range(split, end)))

    place = lax.rem(z, REACH)
    tail = place == REACH - 1

    def inside(d):
        return jnp.logical_and(feeds(d), place + d < REACH)

    def feeds(d):
        return jnp.logical_and(z >= origin, z + d < nz)

    def chip(dx):
        return {"seq": lax.rem(x + dx, nx) * 2 + core}

    partner = {"seq": x * 2 + 1 - core}

    def remote(src, dst, send, recv, where):
        pltpu.make_async_remote_copy(
            src_ref=src, dst_ref=dst, send_sem=send, recv_sem=recv, device_id=where, device_id_type=MESH
        ).start()

    loads = []
    for i, (hbm, buf) in enumerate(((k_hbm, kb), (v_hbm, vb), (q_hbm, qb))):
        for n in range(chunks):
            cols = pl.ds(n * HPC * DH, HPC * DH)
            loads.append(pltpu.make_async_copy(hbm.at[:, cols], buf.at[:, cols], in_sem.at[i, n]))
    for n in range(chunks):
        loads[n].start()
        loads[chunks + n].start()
    for n in range(chunks):
        loads[2 * chunks + n].start()
    gain_load = pltpu.make_async_copy(gain_hbm, gain, gain_sem)
    gain_load.start()

    barrier = pltpu.get_barrier_semaphore()
    pl.semaphore_signal(barrier, inc=1, device_id=partner, device_id_type=MESH)

    @pl.when(jnp.logical_not(first))
    def _():
        for dx in range(1, nx):
            pl.semaphore_signal(barrier, inc=1, device_id=chip(dx), device_id_type=MESH)

    notes = [(feeds(d), z + d) for d in range(1, REACH + 1)]
    @pl.when(odd)
    def _():
        pl.semaphore_signal(barrier, inc=1, device_id={"seq": 0}, device_id_type=MESH)

    notes += [(jnp.logical_and(plane, jnp.logical_and(z >= 1, z <= relay)), 0), (late, end)]
    for there, to in notes:
        @pl.when(there)
        def _():
            pl.semaphore_signal(barrier, inc=1, device_id={"grp": to}, device_id_type=MESH)

    def greeted():
        behind = jnp.minimum(jnp.maximum(z - origin, 0), REACH)
        behind = behind + jnp.where(first, nx - 1, 0) - jnp.where(row, 1, 0)
        pl.semaphore_wait(barrier, nx + behind + jnp.where(late, relay, 0) + jnp.where(final, 1, 0))
        for d in range(1, REACH + 1):
            @pl.when(z - d >= origin)
            def _():
                pl.semaphore_signal(hello.at[d - 1], inc=1, device_id={"grp": z - d}, device_id_type=MESH)

        @pl.when(final)
        def _():
            pl.semaphore_signal(word, inc=1, device_id={"grp": 0}, device_id_type=MESH)

        @pl.when(first)
        def _():
            for i in range(1, nx):
                pl.semaphore_signal(enter, inc=1, device_id={"seq": 2 * i}, device_id_type=MESH)

    def learn(d, wanted):
        @pl.when(jnp.logical_and(feeds(d), wanted))
        def _():
            pl.semaphore_wait(hello.at[d - 1], 1)

    def head(h):
        return pl.ds(h * DH, DH)

    later = lax.broadcasted_iota(jnp.int32, (rows, rows), 0) >= lax.broadcasted_iota(jnp.int32, (rows, rows), 1)

    def local_attention(h):
        cut = pl.ds(pl.multiple_of(h * DH, DH), DH)
        for r in range(2):
            part = pl.ds(r * rows, rows)
            qr = qb[part, cut]
            own_scores = lax.dot_general(qr, kb[part, cut], (((1,), (1,)), ((), ())), preferred_element_type=jnp.float32)
            weights = jnp.where(later, own_scores, 0.0).astype(jnp.bfloat16)
            acc = jnp.dot(weights, vb[part, cut], preferred_element_type=jnp.float32)
            if r == 1:
                top = pl.ds(0, rows)
                full = lax.dot_general(qr, kb[top, cut], (((1,), (1,)), ((), ())), preferred_element_type=jnp.float32)
                acc = acc + jnp.dot(full.astype(jnp.bfloat16), vb[top, cut], preferred_element_type=jnp.float32)
            mixed[part, cut] = acc

    heads_here = chunks * HPC

    def attend(start=0, stop=heads_here):
        @pl.loop(start, stop)
        def _(h):
            local_attention(h)

    def fill(part):
        @pl.when(jnp.logical_not(late))
        def _():
            attend(heads_here * FILL[part] // 6, heads_here * FILL[part + 1] // 6)

    def exchange(n):
        remote(kv.at[n], pk.at[n], sc.at[n], rc.at[n], partner)

    def make(n):
        loads[n].wait()
        loads[chunks + n].wait()
        for j in range(HPC):
            cut = head(n * HPC + j)
            kv[n, pl.ds(j * DH, DH), :] = lax.dot_general(
                kb[:, cut], vb[:, cut], (((0,), (0,)), ((), ())), preferred_element_type=jnp.float32
            )

    waits = jnp.logical_and(late, jnp.logical_not(first))

    @pl.when(waits)
    def _():
        for n in range(chunks):
            make(n)
        for load in loads[2 * chunks:]:
            load.wait()
        attend()
        greeted()
        for n in range(chunks):
            exchange(n)

    @pl.when(jnp.logical_not(waits))
    def _():
        for n in range(chunks):
            if n == 0:
                @pl.when(first)
                def _():
                    greeted()

            make(n)
            if n == 0:
                @pl.when(jnp.logical_not(first))
                def _():
                    greeted()

            @pl.when(first)
            def _():
                for i in (2, 1, 3, 0):
                    remote(kv.at[n, pl.ds(half + i * slc, slc)], lk.at[n], sk.at[n, i], rk.at[n], {"seq": 2 * i + 1})

            exchange(n)
        for load in loads[2 * chunks:]:
            load.wait()

    gain_load.wait()
    def arrives(d):
        return jnp.logical_and(place >= d, z - d >= origin)

    for i, full in (*((d - 1, arrives(d)) for d in range(1, REACH)), (REACH - 1, z >= REACH)):
        @pl.when(jnp.logical_not(full))
        def _():
            for n in range(chunks):
                rw[n, i] = jnp.zeros((slc, DH), jnp.float32)

    mine = pl.ds(core * half, half)
    for n in range(chunks):
        @pl.when(mate)
        def _():
            ts[n] = kv[n, mine, :]

        @pl.when(jnp.logical_not(mate))
        def _():
            take(rc.at[n], pk.at[n])
            ts[n] = kv[n, mine, :] + pk[n, mine, :]

        for dx in (2, 1, 3):
            to = lax.rem(x + dx, nx)

            @pl.when(jnp.logical_not(jnp.logical_and(row, to == 0)))
            def _():
                remote(ts.at[n, pl.ds(to * slc, slc)], ra.at[n, pl.ds(x * slc, slc)], sa.at[n], rcv_a.at[n], chip(dx))

        ra[n, pl.ds(x * slc, slc), :] = ts[n, pl.ds(x * slc, slc), :]

    @pl.when(row)
    def _():
        pl.semaphore_wait(enter, 1)
        for n in range(chunks):
            remote(ts.at[n, pl.ds(0, slc)], ra.at[n, pl.ds(x * slc, slc)], sa.at[n], rcv_a.at[n], {"seq": 0})

    fill(0)

    for n in range(chunks):
        take(rcv_a.at[n], ra.at[n, pl.ds(0, (nx - 1) * slc)])

        @pl.when(jnp.logical_and(late, core == 1))
        def _():
            take(rk.at[n], lk.at[n])
            ra[n, pl.ds(0, slc), :] = ra[n, pl.ds(0, slc), :] + lk[n]

        total = ra[n, pl.ds(0, slc), :]
        for i in range(1, nx):
            total = total + ra[n, pl.ds(i * slc, slc), :]
        gs[n] = total
        for d in range(1, REACH):
            if n == 0:
                learn(d, place + d < REACH)

            @pl.when(inside(d))
            def _():
                remote(gs.at[n], rw.at[n, d - 1], s1.at[n, d - 1], r1.at[n, d - 1], {"grp": z + d})

        @pl.when(late)
        def _():
            for i, to in enumerate((1, 2, relay)):
                remote(gs.at[n], lt.at[n], sl.at[n, i], rl.at[n], {"grp": to})


    @pl.when(late)
    def _():
        pl.semaphore_wait(word, 1)
        for n in range(chunks):
            for i, to in enumerate((*range(3, relay), end)):
                remote(gs.at[n], lt.at[n], sl.at[n, 3 + i], rl.at[n], {"grp": to})

    def pass_on(n, source, targets):
        @pl.when(z == source)
        def _():
            for i, to in enumerate(targets):
                remote(lt.at[n], lt.at[n], sl.at[n, i], rl.at[n], {"grp": to})

    @pl.when(final)
    def _():
        for n in range(chunks):
            take(rl.at[n], lt.at[n])
            pass_on(n, *fans[-1])

    fill(1)


    def hand_back(n, before):
        for i in range(nx):
            cs[n, pl.ds(i * slc, slc), :] = before
            before = before + ra[n, pl.ds(i * slc, slc), :]
        land = pl.ds(core * half + x * slc, slc)
        for dx in (2, 1, 3):
            to = lax.rem(x + dx, nx)
            remote(cs.at[n, pl.ds(to * slc, slc)], rf.at[n, land], s3.at[n], r3.at[n], chip(dx))
        rf[n, land, :] = cs[n, pl.ds(x * slc, slc), :]

    for n in range(chunks):
        for d in range(1, REACH):
            @pl.when(arrives(d))
            def _():
                take(r1.at[n, d - 1], rw.at[n, d - 1])

        near = rw[n, 0] + rw[n, 1] + rw[n, 2]

        @pl.when(z >= REACH)
        def _():
            take(r1.at[n, REACH - 1], rw.at[n, REACH - 1])

        before = rw[n, REACH - 1] + near
        run[n] = before + gs[n]
        for d in (REACH, *range(1, REACH)):
            if n == 0:
                learn(d, tail)

            @pl.when(jnp.logical_and(feeds(d), tail))
            def _():
                remote(run.at[n], rw.at[n, REACH - 1], s1.at[n, d - 1], r1.at[n, REACH - 1], {"grp": z + d})

        bf[n] = before

        @pl.when(jnp.logical_not(plane))
        def _():
            hand_back(n, bf[n])

    for d in range(1, REACH + 1):
        learn(d, jnp.logical_and(place + d >= REACH, jnp.logical_not(tail)))

    @pl.when(plane)
    def _():
        for n in range(chunks):
            @pl.when(jnp.logical_and(z >= 1, z < end))
            def _():
                take(rl.at[n], lt.at[n])
                for source, targets in fans[:-1]:
                    pass_on(n, source, targets)

            @pl.when(z >= 1)
            def _():
                bf[n] = bf[n] + lt[n]

            hand_back(n, bf[n])

    fill(2)
    for n in range(chunks):
        take(r3.at[n], rf.at[n, pl.ds(0, (nx - 1) * slc)])
        remote(rf.at[n, mine], rf.at[n, mine], s4.at[n], r4.at[n], partner)

    @pl.when(first)
    def _():
        attend()

    @pl.when(mate)
    def _():
        for n in range(chunks):
            take(rc.at[n], pk.at[n])

    for n in range(chunks):
        take(sc.at[n], kv.at[n])
        take(sa.at[n], ts.at[n, pl.ds(0, (nx - 1) * slc)])
        take(s3.at[n], cs.at[n, pl.ds(0, (nx - 1) * slc)])

        for d in range(1, REACH + 1):
            @pl.when(jnp.logical_and(feeds(d), jnp.logical_or(tail, place + d < REACH)))
            def _():
                take(s1.at[n, d - 1], gs.at[n])

        @pl.when(first)
        def _():
            for i in range(nx):
                take(sk.at[n, i], lk.at[n])

        @pl.when(late)
        def _():
            for i in range(relay + 1):
                take(sl.at[n, i], lt.at[n])

        for source, targets in fans:
            @pl.when(jnp.logical_and(plane, z == source))
            def _():
                for i in range(len(targets)):
                    take(sl.at[n, i], lt.at[n])

    second = core == 1

    def finish(n, j):
        cut = pl.ds(pl.multiple_of((n * HPC + j) * DH, DH), DH)
        at = pl.ds(pl.multiple_of(j * DH, DH), DH)
        state = rf[n, at, :] + jnp.where(second, pk[n, at, :], 0.0)
        m = mixed[:, cut] + jnp.dot(qb[:, cut], state.astype(jnp.bfloat16), preferred_element_type=jnp.float32)
        meansq = jnp.mean(m * m, axis=-1, keepdims=True)
        scale = gain[head(n * HPC)]
        for i in range(1, HPC):
            scale = jnp.where(j == i, gain[head(n * HPC + i)], scale)
        out_ref[:, cut] = (m * lax.rsqrt(meansq + eps) * scale.reshape(1, DH)).astype(jnp.bfloat16)

    for n in range(chunks):
        finish(n, (HPC - 1) * core)
    for n in range(chunks):
        take(r4.at[n], rf.at[n, pl.ds(0, half)])
        for i in range(1, HPC - 1):
            finish(n, i)
        finish(n, (HPC - 1) * (1 - core))

    for n in range(chunks):
        take(s4.at[n], rf.at[n, pl.ds(0, half)])


def per_device(query_feat, key_feat, value_feat, norm_gain):
    tokens, width = query_feat.shape[2:]
    nx, nz = lax.axis_size("seq") // 2, lax.axis_size("grp")
    chunks = width // (HPC * DH)
    half = HPC * DH // 2
    slc = half // nx
    f32 = jnp.float32
    dma = pltpu.SemaphoreType.DMA

    def kernel(*refs):
        body(nx, nz, 1e-05, *refs)

    hbm = pl.BlockSpec(memory_space=pltpu.HBM)
    vmem = pl.BlockSpec(memory_space=pltpu.VMEM)
    out = pl.pallas_call(
        kernel,
        out_shape=jax.ShapeDtypeStruct((tokens, width), jnp.bfloat16),
        in_specs=[hbm, hbm, hbm, hbm],
        out_specs=vmem,
        scratch_shapes=[
            pltpu.VMEM((tokens, width), jnp.bfloat16),
            pltpu.VMEM((tokens, width), jnp.bfloat16),
            pltpu.VMEM((tokens, width), jnp.bfloat16),
            pltpu.VMEM((width,), f32),
            pltpu.VMEM((tokens, width), f32),
            pltpu.VMEM((chunks, HPC * DH, DH), f32),
            pltpu.VMEM((chunks, HPC * DH, DH), f32),
            pltpu.VMEM((chunks, half, DH), f32),
            pltpu.VMEM((chunks, half, DH), f32),
            pltpu.VMEM((chunks, slc, DH), f32),
            pltpu.VMEM((chunks, REACH, slc, DH), f32),
            pltpu.VMEM((chunks, slc, DH), f32),
            pltpu.VMEM((chunks, slc, DH), f32),
            pltpu.VMEM((chunks, slc, DH), f32),
            pltpu.VMEM((chunks, slc, DH), f32),
            pltpu.VMEM((chunks, half, DH), f32),
            pltpu.VMEM((chunks, HPC * DH, DH), f32),
            dma((3, chunks)), dma,
            dma((chunks,)), dma((chunks,)),
            dma((chunks,)), dma((chunks,)),
            dma((chunks, REACH)), dma((chunks, REACH)),
            dma((chunks,)), dma((chunks,)),
            dma((chunks,)), dma((chunks,)),
            dma((chunks, nz)), dma((chunks,)),
            dma((chunks, nx)), dma((chunks,)),
            pltpu.SemaphoreType.REGULAR((REACH,)),
            pltpu.SemaphoreType.REGULAR,
            pltpu.SemaphoreType.REGULAR,
        ],
        compiler_params=pltpu.CompilerParams(collective_id=0, has_side_effects=True, vmem_limit_bytes=48 * 1024 * 1024),
        name="prefix_attention",
    )(
        *(
            pltpu.with_memory_space_constraint(a, pltpu.HBM)
            for a in (
                query_feat.reshape(tokens, width),
                key_feat.reshape(tokens, width),
                value_feat.reshape(tokens, width),
                norm_gain,
            )
        )
    )
    return out.reshape(query_feat.shape)


def solution(mesh):
    placed = (
        P("grp", "seq", None, "head"),
        P("grp", "seq", None, "head"),
        P("grp", "seq", None, "head"),
        P("head"),
    )
    return jax.shard_map(
        per_device,
        mesh=mesh,
        in_specs=placed,
        out_specs=P("grp", "seq", None, "head"),
        check_vma=False,
    )
```
